32 devices in a mesh: blk: 8 (over y, x, core), seq: 4 (over z).
Axes of the slice: x: 2, y: 2, z: 4, core: 2. Of those that a mesh axis runs over, the one named last changes fastest.
Arguments:
- layer_input: bfloat16 [8, 512, 8192], P('blk', 'seq'), may hold values from -6 to 6
- queries: bfloat16 [8, 512, 4096], P('blk', 'seq'), may hold values from -48 to 48, as said below
- grad_out: bfloat16 [8, 512, 4096], P('blk', 'seq'), may hold values from -6 to 6
- segment_ids: int32 [8, 512], P('blk', 'seq'), may hold values from 0 to 3, never falling along the last dimension, each value on 1 to 256 neighbouring positions
- kv_weight: bfloat16 [8192, 1024], P(('blk', 'seq')), may hold values from -0.0625 to 0.0625
- norm_gain: float32 [8192], replicated, may hold values from 0.5 to 1.5
Outputs:
- attended: bfloat16 [8, 512, 4096], P('blk', 'seq')
- grad_queries: bfloat16 [8, 512, 4096], P('blk', 'seq')
- grad_input: bfloat16 [8, 512, 8192], P('blk', 'seq')
- grad_weight: float32 [8192, 1024], P(('blk', 'seq'))
- grad_gain: float32 [8192], replicated
The draws below stay inside these ranges and needn't reach their ends.
Inputs may be any that keep to these rules, and one draw needn't show every extreme that they name: Projected queries; some rows may be larger than others.
All inputs are finite; a program needn't handle non-finite values.
Results may differ from the reference program's by a relative error of at most 0.02.
The reference program's roundings to bfloat16 on the way count: a program that leaves them out, or rounds other values in their place, can miss the bound.
Values may be sent and summed in bfloat16 or wider, within the bound.
A program may use at most 128 MiB of HBM per device.

```python
import math
import jax
import jax.numpy as jnp
import numpy as np
from jax import lax

D = 8192
HEAD = 128
KV_HEADS = 4
Q_HEADS = 32
LENGTH = 512
QW = 4096
KVC = 1024
N_BLK = 8


def draw_queries(key, part):
    base = jax.random.normal(key, (N_BLK, LENGTH, QW), jnp.float32)
    base = jnp.clip(base, -4.0, 4.0)
    return base.astype(jnp.bfloat16)


def block_levels(rng, dims, cuts, smallest, top_value):
    def one(axis_at, shards_of):
        heights = jax.random.uniform(jax.random.fold_in(jax.random.fold_in(rng, 6), axis_at), (shards_of,), jnp.float32, smallest / len(cuts), top_value / len(cuts))
        return jnp.repeat(jnp.exp(heights), dims[axis_at] // shards_of).reshape((-1,) + (1,) * (len(dims) - axis_at - 1))

    level = one(*cuts[0])
    for cut in cuts[1:]:
        level = level * one(*cut)
    return level


def length_profile(amount, total, bound, slope):
    loads = [(1 << 20) // math.isqrt(standing ** slope) + 1 for standing in range(2, amount + 1)]
    surplus, given = total - bound - (amount - 1), [1] * (amount - 1)
    while surplus > 0:
        movable = [i for i in range(amount - 1) if given[i] < bound]
        whole, budget = sum([loads[i] for i in movable]), surplus
        for i in movable:
            more = min(bound - given[i], max(1, budget * loads[i] // whole), surplus)
            given[i] = given[i] + more
            surplus = surplus - more
    return np.array([bound] + given)


def uneven_parts(rng, amount, total, limit, lean):
    if amount == 2:
        one = jax.random.randint(rng, (), max(1, total - limit), min(limit, total - 1) + 1)
        return jnp.stack([one, total - one])
    sizes = jnp.asarray(length_profile(amount, total, limit, lean), jnp.int32)
    pairs = (amount - 1) // 2
    donor, taker = sizes[1:1 + 2 * pairs:2], sizes[2:2 + 2 * pairs:2]
    slack = jnp.minimum(donor - 1, limit - taker)
    passed = jax.random.randint(jax.random.fold_in(rng, 1), (pairs,), 0, 1 << 20) % (slack + 1)
    sizes = sizes.at[1:1 + 2 * pairs:2].set(donor - passed).at[2:2 + 2 * pairs:2].set(taker + passed)
    return sizes[jax.random.permutation(jax.random.fold_in(rng, 2), amount)]


def bell_draw(stream_key, dims, width, most, shards=(), dtype=jnp.bfloat16):
    drawn = width * jax.random.normal(stream_key, dims, jnp.float32)
    if shards:
        drawn = drawn * block_levels(stream_key, dims, shards, -0.22, 0.18)
    return jnp.clip(drawn, -most, most).astype(dtype)


def setup_inputs(seed: int = 0) -> dict:
    keys = jax.random.split(jax.random.key(seed), 7)
    return {
        "layer_input": bell_draw(keys[0], (N_BLK, LENGTH, D), 1.0, 6.0, ((0, 8), (1, 4))),
        "queries": draw_queries(jax.random.fold_in(keys[6], 71), 0),
        "grad_out": bell_draw(keys[2], (N_BLK, LENGTH, QW), 1.0, 6.0, ((0, 8), (1, 4))),
        "segment_ids": jax.vmap(lambda own: jnp.searchsorted(jnp.cumsum(uneven_parts(own, 4, LENGTH, LENGTH // 2, 2)), jnp.arange(LENGTH), side="right"))(jax.random.split(keys[3], N_BLK)).reshape((N_BLK, LENGTH)).astype(jnp.int32),
        "kv_weight": bell_draw(keys[4], (D, KVC), D ** -0.5, 0.0625, ((0, 32),)),
        "norm_gain": jnp.clip(1.0 + 0.1 * jax.random.normal(keys[5], (D,), jnp.float32), 0.5, 1.5),
    }


epsilon = 1e-05

def per_sequence(layer_row, query_row, grad_row, segment_row, kv_weight, norm_gain):
    f32 = jnp.float32
    kv_width = KV_HEADS * HEAD
    group_size = Q_HEADS // KV_HEADS
    score_scale = HEAD ** (-0.5)
    source = layer_row.astype(f32)
    inv_rms = lax.rsqrt(lax.optimization_barrier(jnp.mean(source * source, axis=1, keepdims=True)) + epsilon)
    scaled = source * inv_rms
    normed = (scaled * norm_gain).astype(jnp.bfloat16)
    kv_rows = jnp.dot(normed, kv_weight, preferred_element_type=f32).astype(jnp.bfloat16)
    key_heads = kv_rows[:, :kv_width].reshape(LENGTH, KV_HEADS, HEAD).astype(f32)
    value_heads = kv_rows[:, kv_width:].reshape(LENGTH, KV_HEADS, HEAD).astype(f32)
    query_heads = query_row.reshape(LENGTH, KV_HEADS, group_size, HEAD).astype(f32)
    raw_scores = jnp.einsum('qgjd,kgd->gjqk', query_heads, key_heads) * score_scale
    positions = jnp.arange(LENGTH)
    allowed = (positions[None, :] <= positions[:, None]) & (segment_row[None, :] == segment_row[:, None])
    masked = jnp.where(allowed, raw_scores, -1e+30)
    row_max = lax.optimization_barrier(jnp.max(masked, axis=-1, keepdims=True))
    expo_terms = jnp.where(allowed, jnp.exp(masked - row_max), 0.0)
    row_sum = lax.optimization_barrier(jnp.sum(expo_terms, axis=-1, keepdims=True))
    weights = expo_terms.astype(jnp.bfloat16).astype(f32)
    summed = jnp.einsum('gjqk,kgd->gjqd', weights, value_heads) / row_sum
    attended = summed.transpose(2, 0, 1, 3).reshape(LENGTH, QW).astype(jnp.bfloat16)
    log_total = row_max + jnp.log(row_sum)
    softmax_probs = jnp.where(allowed, jnp.exp(masked - log_total), 0.0)
    grad_heads = grad_row.reshape(LENGTH, KV_HEADS, group_size, HEAD).astype(f32).transpose(1, 2, 0, 3)
    attended_heads = attended.reshape(LENGTH, KV_HEADS, group_size, HEAD).astype(f32).transpose(1, 2, 0, 3)
    row_delta = lax.optimization_barrier(jnp.sum(grad_heads * attended_heads, axis=-1, keepdims=True))
    grad_probs = jnp.einsum('gjqd,kgd->gjqk', grad_heads, value_heads)
    grad_scores = (softmax_probs * (grad_probs - row_delta)).astype(jnp.bfloat16).astype(f32)
    probs_half = softmax_probs.astype(jnp.bfloat16).astype(f32)
    grad_values = jnp.einsum('gjqk,gjqd->kgd', probs_half, grad_heads)
    grad_keys = jnp.einsum('gjqk,qgjd->kgd', grad_scores, query_heads) * score_scale
    grad_query = jnp.einsum('gjqk,kgd->qgjd', grad_scores, key_heads) * score_scale
    grad_query = grad_query.reshape(LENGTH, QW).astype(jnp.bfloat16)
    grad_kv = jnp.concatenate([grad_keys.reshape(LENGTH, kv_width), grad_values.reshape(LENGTH, kv_width)], axis=1).astype(jnp.bfloat16)
    weight_term = lax.dot_general(normed, grad_kv, (((0,), (0,)), ((), ())), preferred_element_type=f32)
    grad_normed = lax.dot_general(grad_kv, kv_weight, (((1,), (1,)), ((), ())), preferred_element_type=f32).astype(jnp.bfloat16)
    grad_norm = grad_normed.astype(f32)
    gain_term = lax.optimization_barrier(jnp.sum(grad_norm * scaled, axis=0))
    grad_hat = grad_norm * norm_gain
    grad_input = inv_rms * (grad_hat - scaled * lax.optimization_barrier(jnp.mean(grad_hat * scaled, axis=1, keepdims=True)))
    return (attended, grad_query, grad_input.astype(jnp.bfloat16), weight_term, gain_term)

def reference(layer_input, queries, grad_out, segment_ids, kv_weight, norm_gain):

    def apply_one(bundle):
        return per_sequence(bundle[0], bundle[1], bundle[2], bundle[3], kv_weight, norm_gain)
    attended, grad_queries, grad_input, weight_terms, gain_terms = lax.map(apply_one, (layer_input, queries, grad_out, segment_ids))
    return (attended, grad_queries, grad_input, lax.optimization_barrier(jnp.sum(weight_terms, axis=0)), lax.optimization_barrier(jnp.sum(gain_terms, axis=0)))
```

```python
import functools

import jax
import jax.numpy as jnp
from jax import lax
from jax.experimental import pallas as pl
from jax.experimental.pallas import tpu as pltpu
from jax.sharding import PartitionSpec as P

HEAD = 128
EPSILON = 1e-05
F32 = jnp.float32
BF16 = jnp.bfloat16
MESH = pl.DeviceIdType.MESH
VMEM_LIMIT = 60 * 1024 * 1024


def remote(src, dst, send_sem, recv_sem, **where):
    return pltpu.make_async_remote_copy(
        src_ref=src,
        dst_ref=dst,
        send_sem=send_sem,
        recv_sem=recv_sem,
        device_id=where,
        device_id_type=MESH,
    )


def greet(n, m):
    s = lax.axis_index("seq")
    b = lax.axis_index("blk")
    barrier = pltpu.get_barrier_semaphore()
    for j in range(1, n):
        pl.semaphore_signal(
            barrier, inc=1, device_id={"seq": lax.rem(s + j, n)}, device_id_type=MESH
        )
    for j in range(1, m):
        pl.semaphore_signal(
            barrier, inc=1, device_id={"blk": lax.rem(b + j, m)}, device_id_type=MESH
        )
    pl.semaphore_wait(barrier, n - 1 + m - 1)


class Layout:
    def __init__(self, n, m, piece):
        self.n, self.m, self.piece = n, m, piece
        self.wide = m * piece
        self.direct = piece % 128 == 0
        self.unit = piece if self.direct else 256
        self.units = self.wide // self.unit

    def row(self, sp, t):
        return t * self.n + sp if self.direct else sp * self.units + t

    def cols(self, sp, t):
        return pl.ds(pl.multiple_of(self.row(sp, t) * self.unit, 128), self.unit)

    def within(self, t):
        return pl.ds(pl.multiple_of(t * self.unit, 128), self.unit)

    def enter(self, x):
        if self.direct:
            return x
        lead = x.shape[:-1]
        x = x.reshape(lead + (self.m, self.n, self.piece))
        return jnp.swapaxes(x, -3, -2).reshape(lead + (-1,))

    def leave(self, x):
        if self.direct:
            return x
        lead = x.shape[:-1]
        x = x.reshape(lead + (self.n, self.m, self.piece))
        return jnp.swapaxes(x, -3, -2).reshape(lead + (-1,))


def inverse_rms(x_ref, lay):
    tok, width = x_ref.shape

    def one(i, total):
        v = x_ref[:, pl.ds(pl.multiple_of(i * 512, 512), 512)].astype(F32)
        v = v * v
        part = v[:, :128]
        for q in range(1, 4):
            part = part + v[:, q * 128 : (q + 1) * 128]
        return total + part

    total = lax.fori_loop(0, width // 512, one, jnp.zeros((tok, 128), F32))
    return lax.rsqrt(jnp.sum(total, axis=1, keepdims=True) / width + EPSILON)


def far_first(n):
    return sorted(range(1, n), key=lambda j: -min(j, n - j))


def near_first(n):
    return sorted(range(1, n), key=lambda j: min(j, n - j))


def forward_kernel(
    lay, back,
    x_ref, gain_ref, w_ref, doc_ref,
    cols_out, slab_out, kv_ref, docs_ref,
    cols, send, slab, own, psend, precv, kvown,
    wsend, wrecv, fsend, frecv, asend, arecv, rsend, rrecv, ksend, krecv, dsend, drecv, lsem,
):
    n, m, piece = lay.n, lay.m, lay.piece
    s = lax.axis_index("seq")
    b = lax.axis_index("blk")
    partner = b + 1 - 2 * lax.rem(b, 2)
    half = m // 2
    greet(n, m)

    def rows(owner):
        return pl.ds(pl.multiple_of(owner * piece, piece), piece)

    spread = []
    for k in range(1, half):
        copy = remote(
            w_ref, slab.at[rows(b)], wsend.at[k], wrecv.at[k], blk=lax.rem(b + 2 * k, m)
        )
        copy.start()
        spread.append(copy)
    first = remote(w_ref, slab.at[rows(b)], fsend.at[0], frecv.at[0], blk=partner)
    first.start()
    mine = pltpu.make_async_copy(w_ref, slab.at[rows(b)], lsem.at[0])
    mine.start()

    doc_copies = []
    for j in range(1, back + 1):
        copy = remote(
            doc_ref, docs_ref.at[j], dsend.at[j], drecv.at[j], seq=lax.rem(s + j, n)
        )
        doc_copies.append(copy)

        @pl.when(s + j < n)
        def _(copy=copy):
            copy.start()

    inv = inverse_rms(x_ref, lay)

    def normed_into(ref, sp):
        def one(t, carry):
            v = x_ref[:, lay.cols(sp, t)].astype(F32) * inv
            g = gain_ref[pl.ds(lay.row(sp, t), 1), :]
            ref[:, lay.within(t)] = (v * g).astype(BF16)
            return carry

        lax.fori_loop(0, lay.units, one, 0)

    out_copies = []
    for j in far_first(n):
        sp = lax.rem(s + j, n)
        normed_into(send.at[j - 1], sp)
        copy = remote(send.at[j - 1], cols.at[s], asend.at[j], arecv.at[j], seq=sp)
        copy.start()
        out_copies.append(copy)
    normed_into(cols.at[s], s)
    docs_ref[0] = doc_ref[...]
    for j in range(1, back + 1):

        @pl.when(s - j < 0)
        def _(j=j):
            docs_ref[j] = jnp.full(docs_ref.shape[1:], -1, jnp.int32)
            kv_ref[j] = jnp.zeros(kv_ref.shape[1:], BF16)

    mine.wait()
    forwards = []
    for k in range(1, half):
        spread[k - 1].wait_recv()
        shard = slab.at[rows(lax.rem(b - 2 * k + m, m))]
        copy = remote(shard, shard, fsend.at[k], frecv.at[k], blk=partner)
        copy.start()
        forwards.append(copy)
    first.wait_recv()
    for copy in forwards:
        copy.wait_recv()
    keep = [pltpu.make_async_copy(slab, slab_out, lsem.at[0])]
    keep[0].start()

    def project(source, target):
        def one(c, carry):
            at = pl.ds(pl.multiple_of(c * 256, 256), 256)
            target[:, at] = jnp.dot(
                cols[source], slab[:, at], preferred_element_type=F32
            )
            return carry

        lax.fori_loop(0, target.shape[1] // 256, one, 0)

    sums = []
    for j in near_first(n):
        source = lax.rem(s - j + n, n)
        remote(send.at[j - 1], cols.at[source], asend.at[j], arecv.at[j], seq=source).wait_recv()
        project(source, psend.at[j - 1])
        copy = remote(
            psend.at[j - 1], precv.at[j - 1], rsend.at[j], rrecv.at[j], seq=source
        )
        copy.start()
        sums.append(copy)
    keep.append(pltpu.make_async_copy(cols, cols_out, lsem.at[1]))
    keep[1].start()
    project(s, own)
    for copy in sums:
        copy.wait_recv()

    def add_up(c, carry):
        at = pl.ds(pl.multiple_of(c * 256, 256), 256)
        total = own[:, at]
        for j in range(1, n):
            total = total + precv[j - 1, :, at]
        kvown[:, at] = total.astype(BF16)
        return carry

    lax.fori_loop(0, own.shape[1] // 256, add_up, 0)
    kv_copies = []
    for j in range(1, back + 1):
        copy = remote(kvown, kv_ref.at[j], ksend.at[j], krecv.at[j], seq=lax.rem(s + j, n))
        kv_copies.append(copy)

        @pl.when(s + j < n)
        def _(copy=copy):
            copy.start()

    kv_ref[0] = kvown[...]
    for j in range(1, back + 1):

        @pl.when(s - j >= 0)
        def _(j=j):
            kv_copies[j - 1].wait_recv()
            doc_copies[j - 1].wait_recv()

        @pl.when(s + j < n)
        def _(j=j):
            kv_copies[j - 1].wait_send()
            doc_copies[j - 1].wait_send()

    for copy in spread + [first] + forwards + out_copies + sums:
        copy.wait_send()
    for copy in keep:
        copy.wait()


def run_forward(lay, back, x, gain, w, docs):
    n, m, piece = lay.n, lay.m, lay.piece
    tok, kvc = x.shape[0], w.shape[1]
    dma = pltpu.SemaphoreType.DMA
    vmem = pl.BlockSpec(memory_space=pltpu.VMEM)
    hbm = pl.BlockSpec(memory_space=pl.ANY)
    return pl.pallas_call(
        functools.partial(forward_kernel, lay, back),
        name="forward_exchange",
        out_shape=(
            jax.ShapeDtypeStruct((n, tok, lay.wide), BF16),
            jax.ShapeDtypeStruct((lay.wide, kvc), BF16),
            jax.ShapeDtypeStruct((back + 1, tok, kvc), BF16),
            jax.ShapeDtypeStruct((back + 1,) + docs.shape, jnp.int32),
        ),
        in_specs=[vmem] * 4,
        out_specs=(hbm, hbm, vmem, vmem),
        scratch_shapes=[
            pltpu.VMEM((n, tok, lay.wide), BF16),
            pltpu.VMEM((n - 1, tok, lay.wide), BF16),
            pltpu.VMEM((lay.wide, kvc), BF16),
            pltpu.VMEM((tok, kvc), F32),
            pltpu.VMEM((n - 1, tok, kvc), F32),
            pltpu.VMEM((n - 1, tok, kvc), F32),
            pltpu.VMEM((tok, kvc), BF16),
            dma((m // 2,)), dma((m // 2,)), dma((m // 2,)), dma((m // 2,)),
            dma((n,)), dma((n,)), dma((n,)), dma((n,)),
            dma((n,)), dma((n,)), dma((n,)), dma((n,)),
            dma((2,)),
        ],
        compiler_params=pltpu.CompilerParams(
            collective_id=0, has_side_effects=True, vmem_limit_bytes=VMEM_LIMIT
        ),
    )(x, gain, w, docs)


def attention_kernel(
    group, q_ref, g_ref, k_ref, v_ref, docs_ref, doc_ref, att_ref, dq_ref, own_ref, far_ref, dk, dv
):
    slots, tok = k_ref.shape[0], k_ref.shape[1]
    keys = slots * tok
    scale = HEAD ** (-0.5)
    k = k_ref[...].reshape(keys, HEAD)
    v = v_ref[...].reshape(keys, HEAD)
    row = lax.broadcasted_iota(jnp.int32, (tok, tok), 0)
    col = lax.broadcasted_iota(jnp.int32, (tok, tok), 1)
    mine = doc_ref[...]
    parts = [(docs_ref[0, 0:1, :] == mine) & (col <= row)]
    for j in range(1, slots):
        parts.append(docs_ref[j, 0:1, :] == mine)
    bias = jnp.concatenate([jnp.where(p, 1.0, 0.0).astype(F32) for p in parts], axis=1)
    allowed = bias > 0.5
    dk[...] = jnp.zeros_like(dk)
    dv[...] = jnp.zeros_like(dv)
    nt = (((1,), (1,)), ((), ()))
    tn = (((0,), (0,)), ((), ()))

    def head(h, carry):
        at = pl.ds(pl.multiple_of(h * HEAD, HEAD), HEAD)
        q = q_ref[:, at]
        g = g_ref[:, at]
        raw = lax.dot_general(q, k, nt, preferred_element_type=F32) * scale
        masked = jnp.where(allowed, raw, -1e30)
        top = jnp.max(masked, axis=1, keepdims=True)
        expo = jnp.where(allowed, jnp.exp(masked - top), 0.0)
        inv = 1.0 / jnp.sum(expo, axis=1, keepdims=True)
        att = (
            jnp.dot(expo.astype(BF16), v, preferred_element_type=F32) * inv
        ).astype(BF16)
        att_ref[:, at] = att
        delta = jnp.sum(g.astype(F32) * att.astype(F32), axis=1, keepdims=True)
        probs = expo * inv
        gp = lax.dot_general(g, v, nt, preferred_element_type=F32)
        ds = (probs * (gp - delta)).astype(BF16)
        dv[...] += lax.dot_general(probs.astype(BF16), g, tn, preferred_element_type=F32)
        dk[...] += lax.dot_general(ds, q, tn, preferred_element_type=F32)
        dq_ref[:, at] = (
            jnp.dot(ds, k, preferred_element_type=F32) * scale
        ).astype(BF16)
        return carry

    lax.fori_loop(0, group, head, 0, unroll=2)
    own_ref[0] = dk[0:tok, :] * scale
    own_ref[1] = dv[0:tok, :]
    for j in range(1, slots):
        far_ref[j - 1, 0] = (dk[j * tok : (j + 1) * tok, :] * scale).astype(BF16)
        far_ref[j - 1, 1] = dv[j * tok : (j + 1) * tok, :].astype(BF16)


def run_attention(q, g, kv, docs, doc_col):
    slots, tok, kvc = kv.shape
    heads = kvc // 2 // HEAD
    group = q.shape[1] // HEAD // heads
    gw = group * HEAD
    wide = pl.BlockSpec((tok, gw), lambda i: (0, i))
    return pl.pallas_call(
        functools.partial(attention_kernel, group),
        name="attention",
        grid=(heads,),
        out_shape=(
            jax.ShapeDtypeStruct(q.shape, BF16),
            jax.ShapeDtypeStruct(q.shape, BF16),
            jax.ShapeDtypeStruct((2, tok, kvc // 2), F32),
            jax.ShapeDtypeStruct((slots - 1, 2, tok, kvc // 2), BF16),
        ),
        in_specs=[
            wide,
            wide,
            pl.BlockSpec((slots, tok, HEAD), lambda i: (0, 0, i)),
            pl.BlockSpec((slots, tok, HEAD), lambda i: (0, 0, i + heads)),
            pl.BlockSpec(docs.shape, lambda i: (0, 0, 0)),
            pl.BlockSpec(doc_col.shape, lambda i: (0, 0)),
        ],
        out_specs=(
            wide,
            wide,
            pl.BlockSpec((2, tok, HEAD), lambda i: (0, 0, i)),
            pl.BlockSpec((slots - 1, 2, tok, HEAD), lambda i: (0, 0, 0, i)),
        ),
        scratch_shapes=[
            pltpu.VMEM((slots * tok, HEAD), F32),
            pltpu.VMEM((slots * tok, HEAD), F32),
        ],
    )(q, g, kv, kv, docs, doc_col)


def backward_kernel(
    lay, back,
    x_ref, gain_ref, cols_in, slab_in, own_ref, far_ref,
    dx_ref, dw_ref, dgain_ref,
    cols, slab, frecv_buf, gkv, nsend, nrecv, pair_send, pair_recv, keep, osend, orecv, seq_gain, blk_gain,
    psend, precv, gsend, grecv, asend, arecv, csend, crecv, wsend, wrecv, ssend, srecv, bsend, brecv, lsem,
):
    n, m, piece = lay.n, lay.m, lay.piece
    s = lax.axis_index("seq")
    b = lax.axis_index("blk")
    core = lax.rem(b, 2)
    partner = b + 1 - 2 * core
    half = m // 2
    tok, width = x_ref.shape
    kvw = own_ref.shape[2]
    loads = [
        pltpu.make_async_copy(slab_in, slab, lsem.at[0]),
        pltpu.make_async_copy(cols_in, cols, lsem.at[1]),
    ]
    for copy in loads:
        copy.start()
    greet(n, m)
    far_copies = []
    for j in range(1, back + 1):
        copy = remote(
            far_ref.at[j - 1], frecv_buf.at[j - 1], psend.at[j], precv.at[j],
            seq=lax.rem(s - j + n, n),
        )
        far_copies.append(copy)

        @pl.when(s - j >= 0)
        def _(copy=copy):
            copy.start()

        @pl.when(s + j >= n)
        def _(j=j):
            frecv_buf[j - 1] = jnp.zeros(frecv_buf.shape[1:], BF16)

    inv = inverse_rms(x_ref, lay)
    for j in range(1, back + 1):

        @pl.when(s + j < n)
        def _(j=j):
            far_copies[j - 1].wait_recv()

    for part in range(2):
        total = own_ref[part]
        for j in range(1, back + 1):
            total = total + frecv_buf[j - 1, part].astype(F32)
        gkv[s, :, part * kvw : (part + 1) * kvw] = total.astype(BF16)
    gather = []
    for j in far_first(n):
        copy = remote(
            gkv.at[s], gkv.at[s], gsend.at[j], grecv.at[j], seq=lax.rem(s + j, n)
        )
        copy.start()
        gather.append(copy)
    loads[0].wait()

    def to_normed(source, ref):
        def one(t, carry):
            rows = pl.ds(pl.multiple_of(t * lay.unit, lay.unit), lay.unit)
            ref[:, lay.within(t)] = lax.dot_general(
                gkv[source], slab[rows, :], (((1,), (1,)), ((), ())),
                preferred_element_type=F32,
            ).astype(BF16)
            return carry

        lax.fori_loop(0, lay.units, one, 0)

    to_normed(s, nrecv.at[s])
    normed_copies = []
    for j in near_first(n):
        source = lax.rem(s - j + n, n)
        remote(gkv.at[s], gkv.at[source], gsend.at[j], grecv.at[j], seq=source).wait_recv()
        to_normed(source, nsend.at[j - 1])
        copy = remote(nsend.at[j - 1], nrecv.at[s], asend.at[j], arecv.at[j], seq=source)
        copy.start()
        normed_copies.append(copy)
    loads[1].wait()

    def weight_tile(t):
        left = cols[:, :, lay.within(t)].reshape(n * tok, lay.unit)
        return lax.dot_general(
            left, gkv[...].reshape(n * tok, 2 * kvw), (((0,), (0,)), ((), ())),
            preferred_element_type=F32,
        )

    pair_copies = [
        remote(pair_send.at[k], pair_recv.at[k], csend.at[k], crecv.at[k], blk=partner)
        for k in range(half)
    ]
    per = lay.unit // piece
    if per == 1:
        for k in range(half):
            pair_send[k] = weight_tile(2 * k + 1 - core).astype(BF16)
            pair_copies[k].start()

        def kept(k, carry):
            keep[k] = weight_tile(2 * k + core)
            return carry

        lax.fori_loop(0, half, kept, 0)
    else:

        def both(t, carry):
            tile = weight_tile(t)
            for r in range(per):
                part = tile[r * piece : (r + 1) * piece]
                k = (t * per + r) // 2

                @pl.when(core == r % 2)
                def _(part=part, k=k):
                    keep[k] = part

                @pl.when(core != r % 2)
                def _(part=part, k=k):
                    pair_send[k] = part.astype(BF16)

            return carry

        lax.fori_loop(0, lay.units, both, 0)
        for copy in pair_copies:
            copy.start()
    for copy in pair_copies:
        copy.wait_recv()
    place = b // 2
    owner_copies = []
    for k in range(1, half):
        slot = lax.rem(place + k, half)
        osend[k - 1] = (keep[slot] + pair_recv[slot].astype(F32)).astype(BF16)
        copy = remote(
            osend.at[k - 1], orecv.at[k - 1], wsend.at[k], wrecv.at[k], blk=lax.rem(b + 2 * k, m)
        )
        copy.start()
        owner_copies.append(copy)

    for j in near_first(n):
        source = lax.rem(s + j, n)
        remote(nsend.at[j - 1], nrecv.at[source], asend.at[n - j], arecv.at[n - j], seq=source).wait_recv()

    def means(i, total):
        sp = i // lay.units
        t = lax.rem(i, lay.units)
        row = pl.ds(lay.row(sp, t), 1)
        scaled = x_ref[:, lay.cols(sp, t)].astype(F32) * inv
        term = nrecv[sp, :, lay.within(t)].astype(F32) * scaled
        seq_gain[pl.ds(s, 1), row, :] = jnp.sum(term, axis=0, keepdims=True)[None]
        term = term * gain_ref[row, :]
        part = term[:, :128]
        for q in range(1, lay.unit // 128):
            part = part + term[:, q * 128 : (q + 1) * 128]
        return total + part

    total = lax.fori_loop(0, n * lay.units, means, jnp.zeros((tok, 128), F32))
    seq_copies = []
    for j in range(1, n):
        copy = remote(
            seq_gain.at[s], seq_gain.at[s], ssend.at[j], srecv.at[j], seq=lax.rem(s + j, n)
        )
        copy.start()
        seq_copies.append(copy)
    mean = jnp.sum(total, axis=1, keepdims=True) / width

    def finish(i, carry):
        sp = i // lay.units
        t = lax.rem(i, lay.units)
        scaled = x_ref[:, lay.cols(sp, t)].astype(F32) * inv
        hat = nrecv[sp, :, lay.within(t)].astype(F32) * gain_ref[pl.ds(lay.row(sp, t), 1), :]
        dx_ref[:, lay.cols(sp, t)] = (inv * (hat - scaled * mean)).astype(BF16)
        return carry

    lax.fori_loop(0, n * lay.units, finish, 0)
    for j in range(1, n):
        source = lax.rem(s - j + n, n)
        remote(
            seq_gain.at[s], seq_gain.at[source], ssend.at[j], srecv.at[j], seq=source
        ).wait_recv()
    gain_sum = seq_gain[0]
    for i in range(1, n):
        gain_sum = gain_sum + seq_gain[i]
    blk_gain[b] = gain_sum
    blk_copies = []
    for j in range(1, m):
        copy = remote(
            blk_gain.at[b], blk_gain.at[b], bsend.at[j], brecv.at[j], blk=lax.rem(b + j, m)
        )
        copy.start()
        blk_copies.append(copy)
    for copy in owner_copies:
        copy.wait_recv()

    dw = keep[place] + pair_recv[place].astype(F32)
    for k in range(1, half):
        dw = dw + orecv[k - 1].astype(F32)
    dw_ref[...] = dw
    for j in range(1, m):
        source = lax.rem(b - j + m, m)
        remote(
            blk_gain.at[b], blk_gain.at[source], bsend.at[j], brecv.at[j], blk=source
        ).wait_recv()
    gain_sum = blk_gain[0]
    for i in range(1, m):
        gain_sum = gain_sum + blk_gain[i]
    dgain_ref[...] = gain_sum
    for copy in gather + normed_copies + pair_copies + owner_copies + seq_copies + blk_copies:
        copy.wait_send()
    for j in range(1, back + 1):

        @pl.when(s - j >= 0)
        def _(j=j):
            far_copies[j - 1].wait_send()


def run_backward(lay, back, x, gain, cols, slab, own, far):
    n, m, piece = lay.n, lay.m, lay.piece
    tok, width = x.shape
    kvc = slab.shape[1]
    dma = pltpu.SemaphoreType.DMA
    vmem = pl.BlockSpec(memory_space=pltpu.VMEM)
    hbm = pl.BlockSpec(memory_space=pl.ANY)
    half = m // 2
    return pl.pallas_call(
        functools.partial(backward_kernel, lay, back),
        name="backward_exchange",
        out_shape=(
            jax.ShapeDtypeStruct((tok, width), BF16),
            jax.ShapeDtypeStruct((piece, kvc), F32),
            jax.ShapeDtypeStruct(gain.shape, F32),
        ),
        in_specs=[vmem, vmem, hbm, hbm, vmem, vmem],
        out_specs=(vmem, vmem, vmem),
        scratch_shapes=[
            pltpu.VMEM(cols.shape, BF16),
            pltpu.VMEM(slab.shape, BF16),
            pltpu.VMEM(far.shape, BF16),
            pltpu.VMEM((n, tok, kvc), BF16),
            pltpu.VMEM((n - 1, tok, lay.wide), BF16),
            pltpu.VMEM((n, tok, lay.wide), BF16),
            pltpu.VMEM((half, piece, kvc), BF16),
            pltpu.VMEM((half, piece, kvc), BF16),
            pltpu.VMEM((half, piece, kvc), F32),
            pltpu.VMEM((half - 1, piece, kvc), BF16),
            pltpu.VMEM((half - 1, piece, kvc), BF16),
            pltpu.VMEM((n,) + gain.shape, F32),
            pltpu.VMEM((m,) + gain.shape, F32),
            dma((n,)), dma((n,)), dma((n,)), dma((n,)), dma((n,)), dma((n,)),
            dma((half,)), dma((half,)), dma((half,)), dma((half,)),
            dma((n,)), dma((n,)), dma((m,)), dma((m,)),
            dma((2,)),
        ],
        compiler_params=pltpu.CompilerParams(
            collective_id=1, has_side_effects=True, vmem_limit_bytes=VMEM_LIMIT
        ),
    )(x, gain, cols, slab, own, far)


def shards(layer_input, queries, grad_out, segment_ids, kv_weight, norm_gain):
    n, m = lax.axis_size("seq"), lax.axis_size("blk")
    tok = layer_input.shape[1]
    lay = Layout(n, m, kv_weight.shape[0])
    back = max(n // 2, 1)
    x = lay.enter(layer_input[0])
    gain = lay.enter(norm_gain).reshape(-1, lay.unit)
    docs = jnp.broadcast_to(segment_ids, (8, tok))
    doc_col = jnp.broadcast_to(segment_ids[0][:, None], (tok, tok))
    cols, slab, kv, all_docs = run_forward(lay, back, x, gain, kv_weight, docs)
    attended, grad_queries, own, far = run_attention(
        queries[0], grad_out[0], kv, all_docs, doc_col
    )
    dx, dw, dgain = run_backward(lay, back, x, gain, cols, slab, own, far)
    return (
        attended[None],
        grad_queries[None],
        lay.leave(dx)[None],
        dw,
        lay.leave(dgain.reshape(-1)),
    )


def solution(mesh):
    tokens = P("blk", "seq", None)
    rows = P(("blk", "seq"), None)
    return jax.shard_map(
        shards,
        mesh=mesh,
        in_specs=(tokens, tokens, tokens, P("blk", "seq"), rows, P()),
        out_specs=(tokens, tokens, tokens, rows, P()),
        check_vma=False,
    )
```

```python
import functools

import jax
import jax.numpy as jnp
from jax import lax
from jax.experimental import pallas as pl
from jax.experimental.pallas import tpu as pltpu
from jax.sharding import PartitionSpec as P

HEAD = 128
EPSILON = 1e-05
F32 = jnp.float32
BF16 = jnp.bfloat16
MESH = pl.DeviceIdType.MESH
VMEM_LIMIT = 60 * 1024 * 1024


def remote(src, dst, send_sem, recv_sem, **where):
    return pltpu.make_async_remote_copy(
        src_ref=src,
        dst_ref=dst,
        send_sem=send_sem,
        recv_sem=recv_sem,
        device_id=where,
        device_id_type=MESH,
    )


def greet(n, m):
    s = lax.axis_index("seq")
    b = lax.axis_index("blk")
    barrier = pltpu.get_barrier_semaphore()
    for j in range(1, n):
        pl.semaphore_signal(
            barrier, inc=1, device_id={"seq": lax.rem(s + j, n)}, device_id_type=MESH
        )
    for j in range(1, m):
        pl.semaphore_signal(
            barrier, inc=1, device_id={"blk": lax.rem(b + j, m)}, device_id_type=MESH
        )
    pl.semaphore_wait(barrier, n - 1 + m - 1)


def inverse_rms(x_ref):
    tok, width = x_ref.shape

    def one(i, total):
        v = x_ref[:, pl.ds(pl.multiple_of(i * 512, 512), 512)].astype(F32)
        v = v * v
        part = v[:, :128]
        for q in range(1, 4):
            part = part + v[:, q * 128 : (q + 1) * 128]
        return total + part

    total = lax.fori_loop(0, width // 512, one, jnp.zeros((tok, 128), F32))
    return lax.rsqrt(jnp.sum(total, axis=1, keepdims=True) / width + EPSILON)


def far_first(n):
    return sorted(range(1, n), key=lambda j: -min(j, n - j))


def lanes(i, size):
    return pl.ds(pl.multiple_of(i * size, 128), size)


def forward_kernel(
    n, m, back,
    x_ref, gain_ref, w_ref, doc_ref,
    cols_out, slab_out, kv_ref, docs_ref,
    cols, send, slab, own, psend, precv,
    usend, urecv, dsend, drecv, fsend, frecv, asend, arecv, rsend, rrecv, ksend, krecv, osend, orecv, lsem,
):
    piece = w_ref.shape[0]
    wide = cols.shape[2]
    half = m // 2
    s = lax.axis_index("seq")
    b = lax.axis_index("blk")
    core = lax.rem(b, 2)
    chip = b // 2
    partner = b + 1 - 2 * core
    greet(n, m)

    def rows(of_core, of_seq):
        return pl.ds(pl.multiple_of((of_core * n + of_seq) * piece, piece), piece)

    up, down = lax.rem(s + 1, n), lax.rem(s + n - 1, n)
    own_rows = rows(core, s)
    first = remote(w_ref, slab.at[own_rows], fsend.at[0], frecv.at[0], blk=partner)

    def hop(source, sender, sems, i, target):
        at = rows(core, source)
        return remote(slab.at[at] if i else w_ref, slab.at[at], sems[0].at[i], sems[1].at[i], seq=target)

    going_up = [hop(lax.rem(s - i + n, n), s, (usend, urecv), i, up) for i in range(n - 1)]
    going_down = [hop(lax.rem(s + i, n), s, (dsend, drecv), i, down) for i in range(n - 1)]

    @pl.when(s + 1 < n)
    def _():
        going_up[0].start()

    @pl.when(s >= 1)
    def _():
        going_down[0].start()

    first.start()
    mine = pltpu.make_async_copy(w_ref, slab.at[own_rows], lsem.at[0])
    mine.start()

    doc_copies = []
    for j in range(1, back + 1):
        copy = remote(
            doc_ref, docs_ref.at[j], osend.at[j], orecv.at[j], seq=lax.rem(s + j, n)
        )
        doc_copies.append(copy)

        @pl.when(s + j < n)
        def _(copy=copy):
            copy.start()

    inv = inverse_rms(x_ref)
    per = wide // 512

    def normed_into(ref, of_chip):
        def one(t, carry):
            at = lanes(of_chip * per + t, 512)
            v = x_ref[:, at].astype(F32) * inv
            ref[:, lanes(t, 512)] = (v * gain_ref[:, at]).astype(BF16)
            return carry

        lax.fori_loop(0, per, one, 0)

    out_copies = []
    for k in range(1, half):
        normed_into(send.at[k - 1], lax.rem(chip + k, half))
        copy = remote(
            send.at[k - 1], cols.at[chip], asend.at[k], arecv.at[k], blk=lax.rem(b + 2 * k, m)
        )
        copy.start()
        out_copies.append(copy)
    normed_into(cols.at[chip], chip)
    docs_ref[0] = doc_ref[...]
    for j in range(1, back + 1):

        @pl.when(s - j < 0)
        def _(j=j):
            docs_ref[j] = jnp.full(docs_ref.shape[1:], -1, jnp.int32)
            kv_ref[j] = jnp.zeros(kv_ref.shape[1:], BF16)

    mine.wait()
    to_partner = []
    for i in range(1, n):
        for side, sems, chain, at_edge in (
            (-1, (usend, urecv), going_up, s - i >= 0),
            (1, (dsend, drecv), going_down, s + i < n),
        ):
            source = lax.rem(s + side * i + n, n)
            slot = i if side < 0 else n - 1 + i
            shard = slab.at[rows(core, source)]
            copy = remote(shard, shard, fsend.at[slot], frecv.at[slot], blk=partner)
            to_partner.append((copy, at_edge))
            more = (s + 1 < n) if side < 0 else (s >= 1)

            @pl.when(at_edge)
            def _(copy=copy, sems=sems, chain=chain, shard=shard, i=i, more=more, side=side):
                remote(
                    shard, shard, sems[0].at[i - 1], sems[1].at[i - 1], seq=up if side < 0 else down
                ).wait_recv()
                if i < n - 1:

                    @pl.when(more)
                    def _():
                        chain[i].start()

                copy.start()

    first.wait_recv()
    for copy, there in to_partner:

        @pl.when(there)
        def _(copy=copy):
            copy.wait_recv()

    keep = [pltpu.make_async_copy(slab, slab_out, lsem.at[0])]
    keep[0].start()

    def project(source, target):
        def one(t, carry):
            at = lanes(t, 256)
            target[:, at] = jnp.dot(cols[source], slab[:, at], preferred_element_type=F32)
            return carry

        lax.fori_loop(0, target.shape[1] // 256, one, 0)

    sums = []
    for k in range(1, half):
        source = lax.rem(chip - k + half, half)
        back_to = lax.rem(b - 2 * k + m, m)
        remote(send.at[k - 1], cols.at[source], asend.at[k], arecv.at[k], blk=back_to).wait_recv()
        project(source, psend.at[k - 1])
        copy = remote(psend.at[k - 1], precv.at[k - 1], rsend.at[k], rrecv.at[k], blk=back_to)
        copy.start()
        sums.append(copy)
    keep.append(pltpu.make_async_copy(cols, cols_out, lsem.at[1]))
    keep[1].start()
    project(chip, own)
    for copy in sums:
        copy.wait_recv()

    def add_up(t, carry):
        at = lanes(t, 256)
        total = own[:, at]
        for k in range(1, half):
            total = total + precv[k - 1, :, at]
        kv_ref[0, :, at] = total.astype(BF16)
        return carry

    lax.fori_loop(0, own.shape[1] // 256, add_up, 0)
    kv_copies = [
        remote(kv_ref.at[j], kv_ref.at[j + 1], ksend.at[j], krecv.at[j], seq=up)
        for j in range(back)
    ]
    for j in range(back):
        if j:

            @pl.when(s - j >= 0)
            def _(j=j):
                kv_copies[j - 1].wait_recv()

        @pl.when((s - j >= 0) & (s + 1 < n))
        def _(j=j):
            kv_copies[j].start()

    @pl.when(s - back >= 0)
    def _():
        kv_copies[back - 1].wait_recv()

    for j in range(back):

        @pl.when((s - j >= 0) & (s + 1 < n))
        def _(j=j):
            kv_copies[j].wait_send()

    for j in range(1, back + 1):

        @pl.when(s - j >= 0)
        def _(j=j):
            doc_copies[j - 1].wait_recv()

        @pl.when(s + j < n)
        def _(j=j):
            doc_copies[j - 1].wait_send()

    for i in range(n - 1):

        @pl.when((s - i >= 0) & (s + 1 < n))
        def _(i=i):
            going_up[i].wait_send()

        @pl.when((s + i < n) & (s >= 1))
        def _(i=i):
            going_down[i].wait_send()

    for copy, there in to_partner:

        @pl.when(there)
        def _(copy=copy):
            copy.wait_send()

    for copy in [first] + out_copies + sums:
        copy.wait_send()
    for copy in keep:
        copy.wait()


def run_forward(n, m, back, x, gain, w, docs):
    tok, width = x.shape
    piece, kvc = w.shape
    half = m // 2
    wide = width // half
    dma = pltpu.SemaphoreType.DMA
    vmem = pl.BlockSpec(memory_space=pltpu.VMEM)
    hbm = pl.BlockSpec(memory_space=pl.ANY)
    return pl.pallas_call(
        functools.partial(forward_kernel, n, m, back),
        name="forward_exchange",
        out_shape=(
            jax.ShapeDtypeStruct((half, tok, wide), BF16),
            jax.ShapeDtypeStruct((wide, kvc), BF16),
            jax.ShapeDtypeStruct((back + 1, tok, kvc), BF16),
            jax.ShapeDtypeStruct((back + 1,) + docs.shape, jnp.int32),
        ),
        in_specs=[vmem] * 4,
        out_specs=(hbm, hbm, vmem, vmem),
        scratch_shapes=[
            pltpu.VMEM((half, tok, wide), BF16),
            pltpu.VMEM((half - 1, tok, wide), BF16),
            pltpu.VMEM((wide, kvc), BF16),
            pltpu.VMEM((tok, kvc), F32),
            pltpu.VMEM((half - 1, tok, kvc), F32),
            pltpu.VMEM((half - 1, tok, kvc), F32),
            dma((n,)), dma((n,)), dma((n,)), dma((n,)),
            dma((2 * n,)), dma((2 * n,)),
            dma((half,)), dma((half,)), dma((half,)), dma((half,)),
            dma((n,)), dma((n,)), dma((n,)), dma((n,)),
            dma((2,)),
        ],
        compiler_params=pltpu.CompilerParams(
            collective_id=0, has_side_effects=True, vmem_limit_bytes=VMEM_LIMIT
        ),
    )(x, gain, w, docs)


def attention_kernel(
    group, q_ref, g_ref, k_ref, v_ref, docs_ref, doc_ref, att_ref, dq_ref, own_ref, far_ref, dk, dv
):
    slots, tok = k_ref.shape[0], k_ref.shape[1]
    keys = slots * tok
    scale = HEAD ** (-0.5)
    k = k_ref[...].reshape(keys, HEAD)
    v = v_ref[...].reshape(keys, HEAD)
    row = lax.broadcasted_iota(jnp.int32, (tok, tok), 0)
    col = lax.broadcasted_iota(jnp.int32, (tok, tok), 1)
    mine = doc_ref[...]
    parts = [(docs_ref[0, 0:1, :] == mine) & (col <= row)]
    for j in range(1, slots):
        parts.append(docs_ref[j, 0:1, :] == mine)
    bias = jnp.concatenate([jnp.where(p, 1.0, 0.0).astype(F32) for p in parts], axis=1)
    allowed = bias > 0.5
    dk[...] = jnp.zeros_like(dk)
    dv[...] = jnp.zeros_like(dv)
    nt = (((1,), (1,)), ((), ()))
    tn = (((0,), (0,)), ((), ()))

    def head(h, carry):
        at = pl.ds(pl.multiple_of(h * HEAD, HEAD), HEAD)
        q = q_ref[:, at]
        g = g_ref[:, at]
        raw = lax.dot_general(q, k, nt, preferred_element_type=F32) * scale
        masked = jnp.where(allowed, raw, -1e30)
        top = jnp.max(masked, axis=1, keepdims=True)
        expo = jnp.where(allowed, jnp.exp(masked - top), 0.0)
        inv = 1.0 / jnp.sum(expo, axis=1, keepdims=True)
        att = (
            jnp.dot(expo.astype(BF16), v, preferred_element_type=F32) * inv
        ).astype(BF16)
        att_ref[:, at] = att
        delta = jnp.sum(g.astype(F32) * att.astype(F32), axis=1, keepdims=True)
        probs = expo * inv
        gp = lax.dot_general(g, v, nt, preferred_element_type=F32)
        ds = (probs * (gp - delta)).astype(BF16)
        dv[...] += lax.dot_general(probs.astype(BF16), g, tn, preferred_element_type=F32)
        dk[...] += lax.dot_general(ds, q, tn, preferred_element_type=F32)
        dq_ref[:, at] = (
            jnp.dot(ds, k, preferred_element_type=F32) * scale
        ).astype(BF16)
        return carry

    lax.fori_loop(0, group, head, 0, unroll=2)
    own_ref[0] = dk[0:tok, :] * scale
    own_ref[1] = dv[0:tok, :]
    for j in range(1, slots):
        far_ref[j - 1, 0] = (dk[j * tok : (j + 1) * tok, :] * scale).astype(BF16)
        far_ref[j - 1, 1] = dv[j * tok : (j + 1) * tok, :].astype(BF16)


def run_attention(q, g, kv, docs, doc_col):
    slots, tok, kvc = kv.shape
    heads = kvc // 2 // HEAD
    group = q.shape[1] // HEAD // heads
    gw = group * HEAD
    wide = pl.BlockSpec((tok, gw), lambda i: (0, i))
    return pl.pallas_call(
        functools.partial(attention_kernel, group),
        name="attention",
        grid=(heads,),
        out_shape=(
            jax.ShapeDtypeStruct(q.shape, BF16),
            jax.ShapeDtypeStruct(q.shape, BF16),
            jax.ShapeDtypeStruct((2, tok, kvc // 2), F32),
            jax.ShapeDtypeStruct((slots - 1, 2, tok, kvc // 2), BF16),
        ),
        in_specs=[
            wide,
            wide,
            pl.BlockSpec((slots, tok, HEAD), lambda i: (0, 0, i)),
            pl.BlockSpec((slots, tok, HEAD), lambda i: (0, 0, i + heads)),
            pl.BlockSpec(docs.shape, lambda i: (0, 0, 0)),
            pl.BlockSpec(doc_col.shape, lambda i: (0, 0)),
        ],
        out_specs=(
            wide,
            wide,
            pl.BlockSpec((2, tok, HEAD), lambda i: (0, 0, i)),
            pl.BlockSpec((slots - 1, 2, tok, HEAD), lambda i: (0, 0, 0, i)),
        ),
        scratch_shapes=[
            pltpu.VMEM((slots * tok, HEAD), F32),
            pltpu.VMEM((slots * tok, HEAD), F32),
        ],
    )(q, g, kv, kv, docs, doc_col)


def backward_kernel(
    n, m, back,
    x_ref, gain_ref, cols_in, slab_in, own_ref, far_ref,
    dx_ref, dw_ref, dgain_ref,
    cols, slab, far_buf, gkv, nsend, nrecv, pair_send, pair_recv, keep, osend, orecv, seq_gain, blk_gain,
    psend, precv, gsend, grecv, asend, arecv, csend, crecv, wsend, wrecv, ssend, srecv, bsend, brecv, lsem,
):
    piece = dw_ref.shape[0]
    wide = cols.shape[2]
    half = m // 2
    s = lax.axis_index("seq")
    b = lax.axis_index("blk")
    core = lax.rem(b, 2)
    chip = b // 2
    partner = b + 1 - 2 * core
    tok, width = x_ref.shape
    kvw = own_ref.shape[2]
    loads = [
        pltpu.make_async_copy(cols_in, cols, lsem.at[0]),
        pltpu.make_async_copy(slab_in, slab, lsem.at[1]),
    ]
    for copy in loads:
        copy.start()
    greet(n, m)
    far_copies = []
    for j in range(1, back + 1):
        copy = remote(
            far_ref.at[j - 1], far_buf.at[j - 1], psend.at[j], precv.at[j],
            seq=lax.rem(s - j + n, n),
        )
        far_copies.append(copy)

        @pl.when(s - j >= 0)
        def _(copy=copy):
            copy.start()

        @pl.when(s + j >= n)
        def _(j=j):
            far_buf[j - 1] = jnp.zeros(far_buf.shape[1:], BF16)

    inv = inverse_rms(x_ref)
    for j in range(1, back + 1):

        @pl.when(s + j < n)
        def _(j=j):
            far_copies[j - 1].wait_recv()

    for part in range(2):
        total = own_ref[part]
        for j in range(1, back + 1):
            total = total + far_buf[j - 1, part].astype(F32)
        gkv[chip, :, part * kvw : (part + 1) * kvw] = total.astype(BF16)
    gather = []
    for k in range(1, half):
        copy = remote(
            gkv.at[chip], gkv.at[chip], gsend.at[k], grecv.at[k], blk=lax.rem(b + 2 * k, m)
        )
        copy.start()
        gather.append(copy)
    for copy in loads:
        copy.wait()

    def to_normed(source, ref):
        def one(t, carry):
            rows = pl.ds(pl.multiple_of(t * 256, 256), 256)
            ref[:, lanes(t, 256)] = lax.dot_general(
                gkv[source], slab[rows, :], (((1,), (1,)), ((), ())),
                preferred_element_type=F32,
            ).astype(BF16)
            return carry

        lax.fori_loop(0, wide // 256, one, 0)

    to_normed(chip, nrecv.at[chip])
    for k in range(1, half):
        source = lax.rem(chip - k + half, half)
        remote(
            gkv.at[chip], gkv.at[source], gsend.at[k], grecv.at[k], blk=lax.rem(b - 2 * k + m, m)
        ).wait_recv()

    tile = 256
    tiles = n * piece // tile

    def weight_tile(of_core, t):
        left = cols[:, :, lanes(of_core * tiles + t, tile)].reshape(half * tok, tile)
        return lax.dot_general(
            left, gkv[...].reshape(half * tok, 2 * kvw), (((0,), (0,)), ((), ())),
            preferred_element_type=F32,
        )

    pair_copies = []
    for t in range(tiles):
        at = pl.ds(t * tile, tile)
        pair_send[at] = weight_tile(1 - core, t).astype(BF16)
        copy = remote(pair_send.at[at], pair_recv.at[at], csend.at[t], crecv.at[t], blk=partner)
        copy.start()
        pair_copies.append(copy)

    def kept(t, carry):
        keep[pl.ds(pl.multiple_of(t * tile, tile), tile)] = weight_tile(core, t)
        return carry

    lax.fori_loop(0, tiles, kept, 0)
    for copy in pair_copies:
        copy.wait_recv()
    owner_copies = []
    for j in far_first(n):
        target = lax.rem(s + j, n)
        at = pl.ds(pl.multiple_of(target * piece, piece), piece)
        osend[j - 1] = (keep[at] + pair_recv[at].astype(F32)).astype(BF16)
        copy = remote(osend.at[j - 1], orecv.at[j - 1], wsend.at[j], wrecv.at[j], seq=target)
        copy.start()
        owner_copies.append(copy)

    normed_copies = []
    for k in range(1, half):
        source = lax.rem(chip - k + half, half)
        to_normed(source, nsend.at[k - 1])
        copy = remote(
            nsend.at[k - 1], nrecv.at[chip], asend.at[k], arecv.at[k], blk=lax.rem(b - 2 * k + m, m)
        )
        copy.start()
        normed_copies.append(copy)

    for k in range(1, half):
        source = lax.rem(chip + k, half)
        remote(
            nsend.at[k - 1], nrecv.at[source], asend.at[k], arecv.at[k], blk=lax.rem(b + 2 * k, m)
        ).wait_recv()

    per = wide // 256

    def means(i, total):
        at = lanes(i, 256)
        scaled = x_ref[:, at].astype(F32) * inv
        term = nrecv[i // per, :, lanes(lax.rem(i, per), 256)].astype(F32) * scaled
        seq_gain[s, pl.ds(i, 1), :] = jnp.sum(term, axis=0, keepdims=True)
        term = term * gain_ref[:, at]
        return total + term[:, :128] + term[:, 128:]

    total = lax.fori_loop(0, width // 256, means, jnp.zeros((tok, 128), F32))
    seq_copies = []
    for j in range(1, n):
        copy = remote(
            seq_gain.at[s], seq_gain.at[s], ssend.at[j], srecv.at[j], seq=lax.rem(s + j, n)
        )
        copy.start()
        seq_copies.append(copy)
    mean = jnp.sum(total, axis=1, keepdims=True) / width

    def finish(i, carry):
        at = lanes(i, 256)
        scaled = x_ref[:, at].astype(F32) * inv
        hat = nrecv[i // per, :, lanes(lax.rem(i, per), 256)].astype(F32) * gain_ref[:, at]
        dx_ref[:, at] = (inv * (hat - scaled * mean)).astype(BF16)
        return carry

    lax.fori_loop(0, width // 256, finish, 0)
    for j in range(1, n):
        source = lax.rem(s - j + n, n)
        remote(
            seq_gain.at[s], seq_gain.at[source], ssend.at[j], srecv.at[j], seq=source
        ).wait_recv()
    gain_sum = seq_gain[0]
    for i in range(1, n):
        gain_sum = gain_sum + seq_gain[i]
    blk_gain[b] = gain_sum
    blk_copies = []
    for j in range(1, m):
        copy = remote(
            blk_gain.at[b], blk_gain.at[b], bsend.at[j], brecv.at[j], blk=lax.rem(b + j, m)
        )
        copy.start()
        blk_copies.append(copy)
    for copy in owner_copies:
        copy.wait_recv()

    at = pl.ds(pl.multiple_of(s * piece, piece), piece)
    dw = keep[at] + pair_recv[at].astype(F32)
    for j in range(1, n):
        dw = dw + orecv[j - 1].astype(F32)
    dw_ref[...] = dw
    for j in range(1, m):
        source = lax.rem(b - j + m, m)
        remote(
            blk_gain.at[b], blk_gain.at[source], bsend.at[j], brecv.at[j], blk=source
        ).wait_recv()
    gain_sum = blk_gain[0]
    for i in range(1, m):
        gain_sum = gain_sum + blk_gain[i]
    dgain_ref[...] = gain_sum
    for copy in gather + normed_copies + pair_copies + owner_copies + seq_copies + blk_copies:
        copy.wait_send()
    for j in range(1, back + 1):

        @pl.when(s - j >= 0)
        def _(j=j):
            far_copies[j - 1].wait_send()


def run_backward(n, m, back, piece, x, gain, cols, slab, own, far):
    tok, width = x.shape
    wide, kvc = slab.shape
    dma = pltpu.SemaphoreType.DMA
    vmem = pl.BlockSpec(memory_space=pltpu.VMEM)
    hbm = pl.BlockSpec(memory_space=pl.ANY)
    half = m // 2
    gains = (width // 256, 256)
    return pl.pallas_call(
        functools.partial(backward_kernel, n, m, back),
        name="backward_exchange",
        out_shape=(
            jax.ShapeDtypeStruct((tok, width), BF16),
            jax.ShapeDtypeStruct((piece, kvc), F32),
            jax.ShapeDtypeStruct(gains, F32),
        ),
        in_specs=[vmem, vmem, hbm, hbm, vmem, vmem],
        out_specs=(vmem, vmem, vmem),
        scratch_shapes=[
            pltpu.VMEM(cols.shape, BF16),
            pltpu.VMEM(slab.shape, BF16),
            pltpu.VMEM(far.shape, BF16),
            pltpu.VMEM((half, tok, kvc), BF16),
            pltpu.VMEM((half - 1, tok, wide), BF16),
            pltpu.VMEM((half, tok, wide), BF16),
            pltpu.VMEM((n * piece, kvc), BF16),
            pltpu.VMEM((n * piece, kvc), BF16),
            pltpu.VMEM((n * piece, kvc), F32),
            pltpu.VMEM((n - 1, piece, kvc), BF16),
            pltpu.VMEM((n - 1, piece, kvc), BF16),
            pltpu.VMEM((n,) + gains, F32),
            pltpu.VMEM((m,) + gains, F32),
            dma((n,)), dma((n,)), dma((half,)), dma((half,)), dma((half,)), dma((half,)),
            dma((n,)), dma((n,)), dma((n,)), dma((n,)),
            dma((n,)), dma((n,)), dma((m,)), dma((m,)),
            dma((2,)),
        ],
        compiler_params=pltpu.CompilerParams(
            collective_id=1, has_side_effects=True, vmem_limit_bytes=VMEM_LIMIT
        ),
    )(x, gain, cols, slab, own, far)


def shards(layer_input, queries, grad_out, segment_ids, kv_weight, norm_gain):
    n, m = lax.axis_size("seq"), lax.axis_size("blk")
    tok = layer_input.shape[1]
    back = max(n // 2, 1)
    x = layer_input[0]
    gain = norm_gain[None]
    docs = jnp.broadcast_to(segment_ids, (8, tok))
    doc_col = jnp.broadcast_to(segment_ids[0][:, None], (tok, tok))
    cols, slab, kv, all_docs = run_forward(n, m, back, x, gain, kv_weight, docs)
    attended, grad_queries, own, far = run_attention(
        queries[0], grad_out[0], kv, all_docs, doc_col
    )
    dx, dw, dgain = run_backward(
        n, m, back, kv_weight.shape[0], x, gain, cols, slab, own, far
    )
    return attended[None], grad_queries[None], dx[None], dw, dgain.reshape(-1)


def solution(mesh):
    tokens = P("blk", "seq", None)
    rows = P(("blk", "seq"), None)
    return jax.shard_map(
        shards,
        mesh=mesh,
        in_specs=(tokens, tokens, tokens, P("blk", "seq"), rows, P()),
        out_specs=(tokens, tokens, tokens, rows, P()),
        check_vma=False,
    )
```

```python
import functools

import jax
import jax.numpy as jnp
from jax import lax
from jax.experimental import pallas as pl
from jax.experimental.pallas import tpu as pltpu
from jax.sharding import PartitionSpec as P

HEAD = 128
EPSILON = 1e-05
F32 = jnp.float32
BF16 = jnp.bfloat16
MESH = pl.DeviceIdType.MESH
VMEM_LIMIT = 60 * 1024 * 1024


def remote(src, dst, send_sem, recv_sem, **where):
    return pltpu.make_async_remote_copy(
        src_ref=src,
        dst_ref=dst,
        send_sem=send_sem,
        recv_sem=recv_sem,
        device_id=where,
        device_id_type=MESH,
    )


def greet(n, m):
    s = lax.axis_index("seq")
    b = lax.axis_index("blk")
    barrier = pltpu.get_barrier_semaphore()
    for j in range(1, n):
        pl.semaphore_signal(
            barrier, inc=1, device_id={"seq": lax.rem(s + j, n)}, device_id_type=MESH
        )
    for j in range(1, m):
        pl.semaphore_signal(
            barrier, inc=1, device_id={"blk": lax.rem(b + j, m)}, device_id_type=MESH
        )
    pl.semaphore_wait(barrier, n - 1 + m - 1)


def inverse_rms(x_ref):
    tok, width = x_ref.shape

    def one(i, total):
        v = x_ref[:, pl.ds(pl.multiple_of(i * 512, 512), 512)].astype(F32)
        v = v * v
        part = v[:, :128]
        for q in range(1, 4):
            part = part + v[:, q * 128 : (q + 1) * 128]
        return total + part

    total = lax.fori_loop(0, width // 512, one, jnp.zeros((tok, 128), F32))
    return lax.rsqrt(jnp.sum(total, axis=1, keepdims=True) / width + EPSILON)


def far_first(n):
    return sorted(range(1, n), key=lambda j: -min(j, n - j))


def lanes(i, size):
    return pl.ds(pl.multiple_of(i * size, 128), size)


def forward_kernel(
    n, m, back,
    x_ref, gain_ref, w_ref, doc_ref,
    cols_out, slab_out, kv_ref, docs_ref,
    cols, send, slab, own, psend, precv,
    usend, urecv, dsend, drecv, fsend, frecv, asend, arecv, rsend, rrecv, ksend, krecv, osend, orecv, lsem,
):
    piece = w_ref.shape[0]
    wide = cols.shape[2]
    half = m // 2
    s = lax.axis_index("seq")
    b = lax.axis_index("blk")
    core = lax.rem(b, 2)
    chip = b // 2
    partner = b + 1 - 2 * core
    greet(n, m)

    def rows(of_core, of_seq):
        return pl.ds(pl.multiple_of((of_core * n + of_seq) * piece, piece), piece)

    kvw = slab.shape[2]
    up, down = lax.rem(s + 1, n), lax.rem(s + n - 1, n)

    def part(ref, h):
        return ref.at[:, pl.ds(h * kvw, kvw)]

    firsts, mines, going_up, going_down, to_partner = [], [], [], [], []
    for h in range(2):
        own_rows = rows(core, s)
        firsts.append(
            remote(
                part(w_ref, h), slab.at[h, own_rows], fsend.at[h, 0], frecv.at[h, 0], blk=partner
            )
        )
        mines.append(
            pltpu.make_async_copy(part(w_ref, h), slab.at[h, own_rows], lsem.at[2 + h])
        )

        def hop(source, sems, i, target, h=h):
            at = slab.at[h, rows(core, source)]
            return remote(
                at if i else part(w_ref, h), at, sems[0].at[h, i], sems[1].at[h, i], seq=target
            )

        going_up.append(
            [hop(lax.rem(s - i + n, n), (usend, urecv), i, up) for i in range(n - 1)]
        )
        going_down.append(
            [hop(lax.rem(s + i, n), (dsend, drecv), i, down) for i in range(n - 1)]
        )

    def set_out(h):
        @pl.when(s + 1 < n)
        def _():
            going_up[h][0].start()

        @pl.when(s >= 1)
        def _():
            going_down[h][0].start()

        firsts[h].start()
        mines[h].start()

    def pass_on(h):
        there = []
        for i in range(1, n):
            for side, sems, chain, at_edge, more in (
                (-1, (usend, urecv), going_up[h], s - i >= 0, s + 1 < n),
                (1, (dsend, drecv), going_down[h], s + i < n, s >= 1),
            ):
                source = lax.rem(s + side * i + n, n)
                slot = i if side < 0 else n - 1 + i
                shard = slab.at[h, rows(core, source)]
                copy = remote(shard, shard, fsend.at[h, slot], frecv.at[h, slot], blk=partner)
                there.append((copy, at_edge))

                @pl.when(at_edge)
                def _(copy=copy, sems=sems, chain=chain, shard=shard, i=i, more=more, side=side):
                    remote(
                        shard, shard, sems[0].at[h, i - 1], sems[1].at[h, i - 1],
                        seq=up if side < 0 else down,
                    ).wait_recv()
                    if i < n - 1:

                        @pl.when(more)
                        def _():
                            chain[i].start()

                    copy.start()

        to_partner.extend(there)
        return there

    def settle(h, there):
        mines[h].wait()
        firsts[h].wait_recv()
        for copy, at_edge in there:

            @pl.when(at_edge)
            def _(copy=copy):
                copy.wait_recv()

    set_out(0)

    doc_copies = []
    for j in range(1, back + 1):
        copy = remote(
            doc_ref, docs_ref.at[j], osend.at[j], orecv.at[j], seq=lax.rem(s + j, n)
        )
        doc_copies.append(copy)

        @pl.when(s + j < n)
        def _(copy=copy):
            copy.start()

    inv = inverse_rms(x_ref)
    per = wide // 512

    def normed_into(ref, of_chip):
        def one(t, carry):
            at = lanes(of_chip * per + t, 512)
            v = x_ref[:, at].astype(F32) * inv
            ref[:, lanes(t, 512)] = (v * gain_ref[:, at]).astype(BF16)
            return carry

        lax.fori_loop(0, per, one, 0)

    out_copies = []
    for k in range(1, half):
        normed_into(send.at[k - 1], lax.rem(chip + k, half))
        copy = remote(
            send.at[k - 1], cols.at[chip], asend.at[k], arecv.at[k], blk=lax.rem(b + 2 * k, m)
        )
        copy.start()
        out_copies.append(copy)
    normed_into(cols.at[chip], chip)
    docs_ref[0] = doc_ref[...]
    for j in range(1, back + 1):

        @pl.when(s - j < 0)
        def _(j=j):
            docs_ref[j] = jnp.full(docs_ref.shape[1:], -1, jnp.int32)
            kv_ref[j] = jnp.zeros(kv_ref.shape[1:], BF16)

    def project(h, source, target):
        def one(t, carry):
            at = lanes(t, 256)
            target[:, at] = jnp.dot(cols[source], slab[h, :, at], preferred_element_type=F32)
            return carry

        lax.fori_loop(0, kvw // 256, one, 0)

    def arrived(k):
        source = lax.rem(chip - k + half, half)
        return remote(
            send.at[k - 1], cols.at[source], asend.at[k], arecv.at[k], blk=lax.rem(b - 2 * k + m, m)
        )

    sums = []

    def project_half(h):
        sums.append([])
        for k in range(1, half):
            if h == 0:
                arrived(k).wait_recv()
            project(h, lax.rem(chip - k + half, half), psend.at[h, k - 1])
            copy = remote(
                psend.at[h, k - 1], precv.at[h, k - 1], rsend.at[h, k], rrecv.at[h, k],
                blk=lax.rem(b - 2 * k + m, m),
            )
            copy.start()
            sums[h].append(copy)
        project(h, chip, own.at[h])

    kv_copies = [
        [
            remote(kv_ref.at[j, h], kv_ref.at[j + 1, h], ksend.at[h, j], krecv.at[h, j], seq=up)
            for j in range(back)
        ]
        for h in range(2)
    ]

    def add_half(h):
        for copy in sums[h]:
            copy.wait_recv()
        total = own[h]
        for k in range(1, half):
            total = total + precv[h, k - 1]
        kv_ref[0, h] = total.astype(BF16)

        @pl.when(s + 1 < n)
        def _():
            kv_copies[h][0].start()

    there = pass_on(0)
    set_out(1)
    settle(0, there)
    project_half(0)
    keep = [pltpu.make_async_copy(cols, cols_out, lsem.at[1])]
    keep[0].start()
    there = pass_on(1)
    settle(1, there)
    keep.append(pltpu.make_async_copy(slab, slab_out, lsem.at[0]))
    keep[1].start()
    project_half(1)
    add_half(0)
    add_half(1)
    for j in range(1, back + 1):
        for h in range(2):

            @pl.when(s - j >= 0)
            def _(j=j, h=h):
                kv_copies[h][j - 1].wait_recv()
                if j < back:

                    @pl.when(s + 1 < n)
                    def _():
                        kv_copies[h][j].start()

    for j in range(back):

        @pl.when((s - j >= 0) & (s + 1 < n))
        def _(j=j):
            kv_copies[0][j].wait_send()
            kv_copies[1][j].wait_send()

    for j in range(1, back + 1):

        @pl.when(s - j >= 0)
        def _(j=j):
            doc_copies[j - 1].wait_recv()

        @pl.when(s + j < n)
        def _(j=j):
            doc_copies[j - 1].wait_send()

    for i in range(n - 1):

        @pl.when((s - i >= 0) & (s + 1 < n))
        def _(i=i):
            going_up[0][i].wait_send()
            going_up[1][i].wait_send()

        @pl.when((s + i < n) & (s >= 1))
        def _(i=i):
            going_down[0][i].wait_send()
            going_down[1][i].wait_send()

    for copy, there in to_partner:

        @pl.when(there)
        def _(copy=copy):
            copy.wait_send()

    for copy in firsts + out_copies + sums[0] + sums[1]:
        copy.wait_send()
    for copy in keep:
        copy.wait()


def run_forward(n, m, back, x, gain, w, docs):
    tok, width = x.shape
    piece, kvc = w.shape
    half = m // 2
    wide = width // half
    dma = pltpu.SemaphoreType.DMA
    vmem = pl.BlockSpec(memory_space=pltpu.VMEM)
    hbm = pl.BlockSpec(memory_space=pl.ANY)
    return pl.pallas_call(
        functools.partial(forward_kernel, n, m, back),
        name="forward_exchange",
        out_shape=(
            jax.ShapeDtypeStruct((half, tok, wide), BF16),
            jax.ShapeDtypeStruct((2, wide, kvc // 2), BF16),
            jax.ShapeDtypeStruct((back + 1, 2, tok, kvc // 2), BF16),
            jax.ShapeDtypeStruct((back + 1,) + docs.shape, jnp.int32),
        ),
        in_specs=[vmem] * 4,
        out_specs=(hbm, hbm, vmem, vmem),
        scratch_shapes=[
            pltpu.VMEM((half, tok, wide), BF16),
            pltpu.VMEM((half - 1, tok, wide), BF16),
            pltpu.VMEM((2, wide, kvc // 2), BF16),
            pltpu.VMEM((2, tok, kvc // 2), F32),
            pltpu.VMEM((2, half - 1, tok, kvc // 2), F32),
            pltpu.VMEM((2, half - 1, tok, kvc // 2), F32),
            dma((2, n)), dma((2, n)), dma((2, n)), dma((2, n)),
            dma((2, 2 * n)), dma((2, 2 * n)),
            dma((half,)), dma((half,)), dma((2, half)), dma((2, half)),
            dma((2, n)), dma((2, n)), dma((n,)), dma((n,)),
            dma((4,)),
        ],
        compiler_params=pltpu.CompilerParams(
            collective_id=0, has_side_effects=True, vmem_limit_bytes=VMEM_LIMIT
        ),
    )(x, gain, w, docs)


def attention_kernel(
    group, q_ref, g_ref, k_ref, v_ref, docs_ref, doc_ref, att_ref, dq_ref, own_ref, far_ref, dk, dv
):
    slots, tok = k_ref.shape[0], k_ref.shape[2]
    keys = slots * tok
    scale = HEAD ** (-0.5)
    k = k_ref[...].reshape(keys, HEAD)
    v = v_ref[...].reshape(keys, HEAD)
    row = lax.broadcasted_iota(jnp.int32, (tok, tok), 0)
    col = lax.broadcasted_iota(jnp.int32, (tok, tok), 1)
    mine = doc_ref[...]
    parts = [(docs_ref[0, 0:1, :] == mine) & (col <= row)]
    for j in range(1, slots):
        parts.append(docs_ref[j, 0:1, :] == mine)
    bias = jnp.concatenate([jnp.where(p, 1.0, 0.0).astype(F32) for p in parts], axis=1)
    allowed = bias > 0.5
    dk[...] = jnp.zeros_like(dk)
    dv[...] = jnp.zeros_like(dv)
    nt = (((1,), (1,)), ((), ()))
    tn = (((0,), (0,)), ((), ()))

    def head(h, carry):
        at = pl.ds(pl.multiple_of(h * HEAD, HEAD), HEAD)
        q = q_ref[:, at]
        g = g_ref[:, at]
        raw = lax.dot_general(q, k, nt, preferred_element_type=F32) * scale
        masked = jnp.where(allowed, raw, -1e30)
        top = jnp.max(masked, axis=1, keepdims=True)
        expo = jnp.where(allowed, jnp.exp(masked - top), 0.0)
        inv = 1.0 / jnp.sum(expo, axis=1, keepdims=True)
        att = (
            jnp.dot(expo.astype(BF16), v, preferred_element_type=F32) * inv
        ).astype(BF16)
        att_ref[:, at] = att
        delta = jnp.sum(g.astype(F32) * att.astype(F32), axis=1, keepdims=True)
        probs = expo * inv
        gp = lax.dot_general(g, v, nt, preferred_element_type=F32)
        ds = (probs * (gp - delta)).astype(BF16)
        dv[...] += lax.dot_general(probs.astype(BF16), g, tn, preferred_element_type=F32)
        dk[...] += lax.dot_general(ds, q, tn, preferred_element_type=F32)
        dq_ref[:, at] = (
            jnp.dot(ds, k, preferred_element_type=F32) * scale
        ).astype(BF16)
        return carry

    lax.fori_loop(0, group, head, 0, unroll=2)
    own_ref[0] = dk[0:tok, :] * scale
    own_ref[1] = dv[0:tok, :]
    for j in range(1, slots):
        far_ref[j - 1, 0] = (dk[j * tok : (j + 1) * tok, :] * scale).astype(BF16)
        far_ref[j - 1, 1] = dv[j * tok : (j + 1) * tok, :].astype(BF16)


def run_attention(q, g, kv, docs, doc_col):
    slots, _, tok, kvw = kv.shape
    heads = kvw // HEAD
    group = q.shape[1] // HEAD // heads
    gw = group * HEAD
    wide = pl.BlockSpec((tok, gw), lambda i: (0, i))
    return pl.pallas_call(
        functools.partial(attention_kernel, group),
        name="attention",
        grid=(heads,),
        out_shape=(
            jax.ShapeDtypeStruct(q.shape, BF16),
            jax.ShapeDtypeStruct(q.shape, BF16),
            jax.ShapeDtypeStruct((2, tok, kvw), F32),
            jax.ShapeDtypeStruct((slots - 1, 2, tok, kvw), BF16),
        ),
        in_specs=[
            wide,
            wide,
            pl.BlockSpec((slots, 1, tok, HEAD), lambda i: (0, 0, 0, i)),
            pl.BlockSpec((slots, 1, tok, HEAD), lambda i: (0, 1, 0, i)),
            pl.BlockSpec(docs.shape, lambda i: (0, 0, 0)),
            pl.BlockSpec(doc_col.shape, lambda i: (0, 0)),
        ],
        out_specs=(
            wide,
            wide,
            pl.BlockSpec((2, tok, HEAD), lambda i: (0, 0, i)),
            pl.BlockSpec((slots - 1, 2, tok, HEAD), lambda i: (0, 0, 0, i)),
        ),
        scratch_shapes=[
            pltpu.VMEM((slots * tok, HEAD), F32),
            pltpu.VMEM((slots * tok, HEAD), F32),
        ],
    )(q, g, kv, kv, docs, doc_col)


def backward_kernel(
    n, m, back,
    x_ref, gain_ref, cols_in, slab_in, own_ref, far_ref,
    dx_ref, dw_ref, dgain_ref,
    cols, slab, far_buf, gkv, nsend, nrecv, pair_send, pair_recv, keep, osend, orecv, seq_gain, blk_gain,
    psend, precv, gsend, grecv, asend, arecv, csend, crecv, wsend, wrecv, ssend, srecv, bsend, brecv, lsem,
):
    piece = dw_ref.shape[0]
    wide = cols.shape[2]
    half = m // 2
    s = lax.axis_index("seq")
    b = lax.axis_index("blk")
    core = lax.rem(b, 2)
    chip = b // 2
    partner = b + 1 - 2 * core
    tok, width = x_ref.shape
    kvw = own_ref.shape[2]
    loads = [
        pltpu.make_async_copy(cols_in, cols, lsem.at[0]),
        pltpu.make_async_copy(slab_in, slab, lsem.at[1]),
    ]
    for copy in loads:
        copy.start()
    greet(n, m)
    far_copies = []
    for h in range(2):
        far_copies.append([])
        for j in range(1, back + 1):
            copy = remote(
                far_ref.at[j - 1, h], far_buf.at[j - 1, h], psend.at[h, j], precv.at[h, j],
                seq=lax.rem(s - j + n, n),
            )
            far_copies[h].append(copy)

            @pl.when(s - j >= 0)
            def _(copy=copy):
                copy.start()

            @pl.when(s + j >= n)
            def _(j=j, h=h):
                far_buf[j - 1, h] = jnp.zeros(far_buf.shape[2:], BF16)

    inv = inverse_rms(x_ref)
    gather = []

    def sum_half(h):
        for j in range(1, back + 1):

            @pl.when(s + j < n)
            def _(j=j):
                far_copies[h][j - 1].wait_recv()

        total = own_ref[h]
        for j in range(1, back + 1):
            total = total + far_buf[j - 1, h].astype(F32)
        gkv[h, chip] = total.astype(BF16)
        for k in range(1, half):
            copy = remote(
                gkv.at[h, chip], gkv.at[h, chip], gsend.at[h, k], grecv.at[h, k],
                blk=lax.rem(b + 2 * k, m),
            )
            copy.start()
            gather.append(copy)

    tile = 256
    tiles = n * piece // tile

    def weight_tile(h, of_core, t):
        left = cols[:, :, lanes(of_core * tiles + t, tile)].reshape(half * tok, tile)
        return lax.dot_general(
            left, gkv[h].reshape(half * tok, kvw), (((0,), (0,)), ((), ())),
            preferred_element_type=F32,
        )

    pair_copies = [[], []]

    def weight_half(h):
        for k in range(1, half):
            source = lax.rem(chip - k + half, half)
            remote(
                gkv.at[h, chip], gkv.at[h, source], gsend.at[h, k], grecv.at[h, k],
                blk=lax.rem(b - 2 * k + m, m),
            ).wait_recv()
        for t in range(tiles):
            at = pl.ds(t * tile, tile)
            pair_send[h, at] = weight_tile(h, 1 - core, t).astype(BF16)
            copy = remote(
                pair_send.at[h, at], pair_recv.at[h, at], csend.at[h, t], crecv.at[h, t], blk=partner
            )
            copy.start()
            pair_copies[h].append(copy)

        def kept(t, carry):
            at = pl.ds(pl.multiple_of(t * tile, tile), tile)
            keep[h, at] = weight_tile(h, core, t)
            return carry

        lax.fori_loop(0, tiles, kept, 0)

    owner_copies = [[], []]

    def send_half(h):
        for copy in pair_copies[h]:
            copy.wait_recv()
        for j in far_first(n):
            target = lax.rem(s + j, n)
            at = pl.ds(pl.multiple_of(target * piece, piece), piece)
            osend[h, j - 1] = (keep[h, at] + pair_recv[h, at].astype(F32)).astype(BF16)
            copy = remote(
                osend.at[h, j - 1], orecv.at[h, j - 1], wsend.at[h, j], wrecv.at[h, j], seq=target
            )
            copy.start()
            owner_copies[h].append(copy)

    def to_normed(source, ref):
        def one(t, carry):
            rows = pl.ds(pl.multiple_of(t * 256, 256), 256)
            terms = [
                lax.dot_general(
                    gkv[h, source], slab[h, rows, :], (((1,), (1,)), ((), ())),
                    preferred_element_type=F32,
                )
                for h in range(2)
            ]
            ref[:, lanes(t, 256)] = (terms[0] + terms[1]).astype(BF16)
            return carry

        lax.fori_loop(0, wide // 256, one, 0)

    sum_half(0)
    for copy in loads:
        copy.wait()
    weight_half(0)
    sum_half(1)
    send_half(0)
    weight_half(1)
    normed_copies = []
    for k in range(1, half):
        source = lax.rem(chip - k + half, half)
        to_normed(source, nsend.at[k - 1])
        copy = remote(
            nsend.at[k - 1], nrecv.at[chip], asend.at[k], arecv.at[k], blk=lax.rem(b - 2 * k + m, m)
        )
        copy.start()
        normed_copies.append(copy)
    send_half(1)
    to_normed(chip, nrecv.at[chip])

    for k in range(1, half):
        source = lax.rem(chip + k, half)
        remote(
            nsend.at[k - 1], nrecv.at[source], asend.at[k], arecv.at[k], blk=lax.rem(b + 2 * k, m)
        ).wait_recv()

    per = wide // 256

    def means(i, total):
        at = lanes(i, 256)
        scaled = x_ref[:, at].astype(F32) * inv
        term = nrecv[i // per, :, lanes(lax.rem(i, per), 256)].astype(F32) * scaled
        seq_gain[s, pl.ds(i, 1), :] = jnp.sum(term, axis=0, keepdims=True)
        term = term * gain_ref[:, at]
        return total + term[:, :128] + term[:, 128:]

    total = lax.fori_loop(0, width // 256, means, jnp.zeros((tok, 128), F32))
    seq_copies = []
    for j in range(1, n):
        copy = remote(
            seq_gain.at[s], seq_gain.at[s], ssend.at[j], srecv.at[j], seq=lax.rem(s + j, n)
        )
        copy.start()
        seq_copies.append(copy)
    mean = jnp.sum(total, axis=1, keepdims=True) / width

    def finish(i, carry):
        at = lanes(i, 256)
        scaled = x_ref[:, at].astype(F32) * inv
        hat = nrecv[i // per, :, lanes(lax.rem(i, per), 256)].astype(F32) * gain_ref[:, at]
        dx_ref[:, at] = (inv * (hat - scaled * mean)).astype(BF16)
        return carry

    lax.fori_loop(0, width // 256, finish, 0)
    for j in range(1, n):
        source = lax.rem(s - j + n, n)
        remote(
            seq_gain.at[s], seq_gain.at[source], ssend.at[j], srecv.at[j], seq=source
        ).wait_recv()
    gain_sum = seq_gain[0]
    for i in range(1, n):
        gain_sum = gain_sum + seq_gain[i]
    blk_gain[b] = gain_sum
    blk_copies = []
    for j in range(1, m):
        copy = remote(
            blk_gain.at[b], blk_gain.at[b], bsend.at[j], brecv.at[j], blk=lax.rem(b + j, m)
        )
        copy.start()
        blk_copies.append(copy)
    at = pl.ds(pl.multiple_of(s * piece, piece), piece)
    for h in range(2):
        for copy in owner_copies[h]:
            copy.wait_recv()
        dw = keep[h, at] + pair_recv[h, at].astype(F32)
        for j in range(1, n):
            dw = dw + orecv[h, j - 1].astype(F32)
        dw_ref[:, h * kvw : (h + 1) * kvw] = dw
    for j in range(1, m):
        source = lax.rem(b - j + m, m)
        remote(
            blk_gain.at[b], blk_gain.at[source], bsend.at[j], brecv.at[j], blk=source
        ).wait_recv()
    gain_sum = blk_gain[0]
    for i in range(1, m):
        gain_sum = gain_sum + blk_gain[i]
    dgain_ref[...] = gain_sum
    for copy in (
        gather + normed_copies + pair_copies[0] + pair_copies[1]
        + owner_copies[0] + owner_copies[1] + seq_copies + blk_copies
    ):
        copy.wait_send()
    for j in range(1, back + 1):

        @pl.when(s - j >= 0)
        def _(j=j):
            far_copies[0][j - 1].wait_send()
            far_copies[1][j - 1].wait_send()


def run_backward(n, m, back, piece, x, gain, cols, slab, own, far):
    tok, width = x.shape
    _, wide, kvw = slab.shape
    kvc = 2 * kvw
    dma = pltpu.SemaphoreType.DMA
    vmem = pl.BlockSpec(memory_space=pltpu.VMEM)
    hbm = pl.BlockSpec(memory_space=pl.ANY)
    half = m // 2
    gains = (width // 256, 256)
    return pl.pallas_call(
        functools.partial(backward_kernel, n, m, back),
        name="backward_exchange",
        out_shape=(
            jax.ShapeDtypeStruct((tok, width), BF16),
            jax.ShapeDtypeStruct((piece, kvc), F32),
            jax.ShapeDtypeStruct(gains, F32),
        ),
        in_specs=[vmem, vmem, hbm, hbm, vmem, vmem],
        out_specs=(vmem, vmem, vmem),
        scratch_shapes=[
            pltpu.VMEM(cols.shape, BF16),
            pltpu.VMEM(slab.shape, BF16),
            pltpu.VMEM(far.shape, BF16),
            pltpu.VMEM((2, half, tok, kvw), BF16),
            pltpu.VMEM((half - 1, tok, wide), BF16),
            pltpu.VMEM((half, tok, wide), BF16),
            pltpu.VMEM((2, n * piece, kvw), BF16),
            pltpu.VMEM((2, n * piece, kvw), BF16),
            pltpu.VMEM((2, n * piece, kvw), F32),
            pltpu.VMEM((2, n - 1, piece, kvw), BF16),
            pltpu.VMEM((2, n - 1, piece, kvw), BF16),
            pltpu.VMEM((n,) + gains, F32),
            pltpu.VMEM((m,) + gains, F32),
            dma((2, n)), dma((2, n)), dma((2, half)), dma((2, half)), dma((half,)), dma((half,)),
            dma((2, n)), dma((2, n)), dma((2, n)), dma((2, n)),
            dma((n,)), dma((n,)), dma((m,)), dma((m,)),
            dma((2,)),
        ],
        compiler_params=pltpu.CompilerParams(
            collective_id=1, has_side_effects=True, vmem_limit_bytes=VMEM_LIMIT
        ),
    )(x, gain, cols, slab, own, far)


def shards(layer_input, queries, grad_out, segment_ids, kv_weight, norm_gain):
    n, m = lax.axis_size("seq"), lax.axis_size("blk")
    tok = layer_input.shape[1]
    back = max(n // 2, 1)
    x = layer_input[0]
    gain = norm_gain[None]
    docs = jnp.broadcast_to(segment_ids, (8, tok))
    doc_col = jnp.broadcast_to(segment_ids[0][:, None], (tok, tok))
    cols, slab, kv, all_docs = run_forward(n, m, back, x, gain, kv_weight, docs)
    attended, grad_queries, own, far = run_attention(
        queries[0], grad_out[0], kv, all_docs, doc_col
    )
    dx, dw, dgain = run_backward(
        n, m, back, kv_weight.shape[0], x, gain, cols, slab, own, far
    )
    return attended[None], grad_queries[None], dx[None], dw, dgain.reshape(-1)


def solution(mesh):
    tokens = P("blk", "seq", None)
    rows = P(("blk", "seq"), None)
    return jax.shard_map(
        shards,
        mesh=mesh,
        in_specs=(tokens, tokens, tokens, P("blk", "seq"), rows, P()),
        out_specs=(tokens, tokens, tokens, rows, P()),
        check_vma=False,
    )
```

```python
import functools

import jax
import jax.numpy as jnp
from jax import lax
from jax.experimental import pallas as pl
from jax.experimental.pallas import tpu as pltpu
from jax.sharding import PartitionSpec as P

HEAD = 128
EPSILON = 1e-05
F32 = jnp.float32
BF16 = jnp.bfloat16
MESH = pl.DeviceIdType.MESH
VMEM_LIMIT = 60 * 1024 * 1024


def remote(src, dst, send_sem, recv_sem, **where):
    return pltpu.make_async_remote_copy(
        src_ref=src,
        dst_ref=dst,
        send_sem=send_sem,
        recv_sem=recv_sem,
        device_id=where,
        device_id_type=MESH,
    )


def greet(n, m):
    s = lax.axis_index("seq")
    b = lax.axis_index("blk")
    barrier = pltpu.get_barrier_semaphore()
    for j in range(1, n):
        pl.semaphore_signal(
            barrier, inc=1, device_id={"seq": lax.rem(s + j, n)}, device_id_type=MESH
        )
    for j in range(1, m):
        pl.semaphore_signal(
            barrier, inc=1, device_id={"blk": lax.rem(b + j, m)}, device_id_type=MESH
        )
    pl.semaphore_wait(barrier, n - 1 + m - 1)


def inverse_rms(x_ref):
    tok, width = x_ref.shape

    def one(i, total):
        v = x_ref[:, pl.ds(pl.multiple_of(i * 512, 512), 512)].astype(F32)
        v = v * v
        part = v[:, :128]
        for q in range(1, 4):
            part = part + v[:, q * 128 : (q + 1) * 128]
        return total + part

    total = lax.fori_loop(0, width // 512, one, jnp.zeros((tok, 128), F32))
    return lax.rsqrt(jnp.sum(total, axis=1, keepdims=True) / width + EPSILON)


def far_first(n):
    return sorted(range(1, n), key=lambda j: -min(j, n - j))


def lanes(i, size):
    return pl.ds(pl.multiple_of(i * size, 128), size)


def forward_kernel(
    n, m, back,
    x_ref, gain_ref, w_ref, doc_ref,
    cols_out, slab_out, kv_ref, docs_ref,
    cols, send, slab, own, psend, precv,
    usend, urecv, dsend, drecv, fsend, frecv, asend, arecv, rsend, rrecv, ksend, krecv, osend, orecv, lsem,
):
    piece = w_ref.shape[0]
    wide = cols.shape[2]
    half = m // 2
    s = lax.axis_index("seq")
    b = lax.axis_index("blk")
    core = lax.rem(b, 2)
    chip = b // 2
    partner = b + 1 - 2 * core
    greet(n, m)

    def rows(of_core, of_seq):
        return pl.ds(pl.multiple_of((of_core * n + of_seq) * piece, piece), piece)

    kvw = slab.shape[2]
    up, down = lax.rem(s + 1, n), lax.rem(s + n - 1, n)

    def part(ref, h):
        return ref.at[:, pl.ds(h * kvw, kvw)]

    firsts, mines, going_up, going_down, to_partner = [], [], [], [], []
    for h in range(2):
        own_rows = rows(core, s)
        firsts.append(
            remote(
                part(w_ref, h), slab.at[h, own_rows], fsend.at[h, 0], frecv.at[h, 0], blk=partner
            )
        )
        mines.append(
            pltpu.make_async_copy(part(w_ref, h), slab.at[h, own_rows], lsem.at[2 + h])
        )

        def hop(source, sems, i, target, h=h):
            at = slab.at[h, rows(core, source)]
            return remote(
                at if i else part(w_ref, h), at, sems[0].at[h, i], sems[1].at[h, i], seq=target
            )

        going_up.append(
            [hop(lax.rem(s - i + n, n), (usend, urecv), i, up) for i in range(n - 1)]
        )
        going_down.append(
            [hop(lax.rem(s + i, n), (dsend, drecv), i, down) for i in range(n - 1)]
        )

    def set_out(h):
        @pl.when(s + 1 < n)
        def _():
            going_up[h][0].start()

        @pl.when(s >= 1)
        def _():
            going_down[h][0].start()

        firsts[h].start()
        mines[h].start()

    def pass_on(h):
        there = []
        for i in range(1, n):
            for side, sems, chain, at_edge, more in (
                (-1, (usend, urecv), going_up[h], s - i >= 0, s + 1 < n),
                (1, (dsend, drecv), going_down[h], s + i < n, s >= 1),
            ):
                source = lax.rem(s + side * i + n, n)
                slot = i if side < 0 else n - 1 + i
                shard = slab.at[h, rows(core, source)]
                copy = remote(shard, shard, fsend.at[h, slot], frecv.at[h, slot], blk=partner)
                there.append((copy, at_edge))

                @pl.when(at_edge)
                def _(copy=copy, sems=sems, chain=chain, shard=shard, i=i, more=more, side=side):
                    remote(
                        shard, shard, sems[0].at[h, i - 1], sems[1].at[h, i - 1],
                        seq=up if side < 0 else down,
                    ).wait_recv()
                    if i < n - 1:

                        @pl.when(more)
                        def _():
                            chain[i].start()

                    copy.start()

        to_partner.extend(there)
        return there

    def settle(h, there):
        mines[h].wait()
        firsts[h].wait_recv()
        for copy, at_edge in there:

            @pl.when(at_edge)
            def _(copy=copy):
                copy.wait_recv()

    set_out(0)

    doc_copies = []
    for j in range(1, back + 1):
        copy = remote(
            doc_ref, docs_ref.at[j], osend.at[j], orecv.at[j], seq=lax.rem(s + j, n)
        )
        doc_copies.append(copy)

        @pl.when(s + j < n)
        def _(copy=copy):
            copy.start()

    inv = inverse_rms(x_ref)
    per = wide // 512

    def normed_into(ref, of_chip):
        def one(t, carry):
            at = lanes(of_chip * per + t, 512)
            v = x_ref[:, at].astype(F32) * inv
            ref[:, lanes(t, 512)] = (v * gain_ref[:, at]).astype(BF16)
            return carry

        lax.fori_loop(0, per, one, 0)

    out_copies = []
    for k in range(1, half):
        normed_into(send.at[k - 1], lax.rem(chip + k, half))
        copy = remote(
            send.at[k - 1], cols.at[chip], asend.at[k], arecv.at[k], blk=lax.rem(b + 2 * k, m)
        )
        copy.start()
        out_copies.append(copy)
    normed_into(cols.at[chip], chip)
    docs_ref[0] = doc_ref[...]
    for j in range(1, back + 1):

        @pl.when(s - j < 0)
        def _(j=j):
            docs_ref[j] = jnp.full(docs_ref.shape[1:], -1, jnp.int32)
            kv_ref[j] = jnp.zeros(kv_ref.shape[1:], BF16)

    def project(h, source, target):
        def one(t, carry):
            at = lanes(t, 256)
            target[:, at] = jnp.dot(cols[source], slab[h, :, at], preferred_element_type=F32)
            return carry

        lax.fori_loop(0, kvw // 256, one, 0)

    def arrived(k):
        source = lax.rem(chip - k + half, half)
        return remote(
            send.at[k - 1], cols.at[source], asend.at[k], arecv.at[k], blk=lax.rem(b - 2 * k + m, m)
        )

    sums = []

    def project_half(h):
        sums.append([])
        for k in range(1, half):
            if h == 0:
                arrived(k).wait_recv()
            project(h, lax.rem(chip - k + half, half), psend.at[h, k - 1])
            copy = remote(
                psend.at[h, k - 1], precv.at[h, k - 1], rsend.at[h, k], rrecv.at[h, k],
                blk=lax.rem(b - 2 * k + m, m),
            )
            copy.start()
            sums[h].append(copy)
        project(h, chip, own.at[h])

    kv_copies = [
        [
            remote(kv_ref.at[j, h], kv_ref.at[j + 1, h], ksend.at[h, j], krecv.at[h, j], seq=up)
            for j in range(back)
        ]
        for h in range(2)
    ]

    def add_half(h):
        for copy in sums[h]:
            copy.wait_recv()
        total = own[h]
        for k in range(1, half):
            total = total + precv[h, k - 1]
        kv_ref[0, h] = total.astype(BF16)

        @pl.when(s + 1 < n)
        def _():
            kv_copies[h][0].start()

    there = pass_on(0)
    set_out(1)
    settle(0, there)
    project_half(0)
    keep = [pltpu.make_async_copy(cols, cols_out, lsem.at[1])]
    keep[0].start()
    there = pass_on(1)
    settle(1, there)
    keep.append(pltpu.make_async_copy(slab, slab_out, lsem.at[0]))
    keep[1].start()
    project_half(1)
    add_half(0)
    add_half(1)
    for j in range(1, back + 1):
        for h in range(2):

            @pl.when(s - j >= 0)
            def _(j=j, h=h):
                kv_copies[h][j - 1].wait_recv()
                if j < back:

                    @pl.when(s + 1 < n)
                    def _():
                        kv_copies[h][j].start()

    for j in range(back):

        @pl.when((s - j >= 0) & (s + 1 < n))
        def _(j=j):
            kv_copies[0][j].wait_send()
            kv_copies[1][j].wait_send()

    for j in range(1, back + 1):

        @pl.when(s - j >= 0)
        def _(j=j):
            doc_copies[j - 1].wait_recv()

        @pl.when(s + j < n)
        def _(j=j):
            doc_copies[j - 1].wait_send()

    for i in range(n - 1):

        @pl.when((s - i >= 0) & (s + 1 < n))
        def _(i=i):
            going_up[0][i].wait_send()
            going_up[1][i].wait_send()

        @pl.when((s + i < n) & (s >= 1))
        def _(i=i):
            going_down[0][i].wait_send()
            going_down[1][i].wait_send()

    for copy, there in to_partner:

        @pl.when(there)
        def _(copy=copy):
            copy.wait_send()

    for copy in firsts + out_copies + sums[0] + sums[1]:
        copy.wait_send()
    for copy in keep:
        copy.wait()


def run_forward(n, m, back, x, gain, w, docs):
    tok, width = x.shape
    piece, kvc = w.shape
    half = m // 2
    wide = width // half
    dma = pltpu.SemaphoreType.DMA
    vmem = pl.BlockSpec(memory_space=pltpu.VMEM)
    hbm = pl.BlockSpec(memory_space=pl.ANY)
    return pl.pallas_call(
        functools.partial(forward_kernel, n, m, back),
        name="forward_exchange",
        out_shape=(
            jax.ShapeDtypeStruct((half, tok, wide), BF16),
            jax.ShapeDtypeStruct((2, wide, kvc // 2), BF16),
            jax.ShapeDtypeStruct((back + 1, 2, tok, kvc // 2), BF16),
            jax.ShapeDtypeStruct((back + 1,) + docs.shape, jnp.int32),
        ),
        in_specs=[vmem] * 4,
        out_specs=(hbm, hbm, vmem, vmem),
        scratch_shapes=[
            pltpu.VMEM((half, tok, wide), BF16),
            pltpu.VMEM((half - 1, tok, wide), BF16),
            pltpu.VMEM((2, wide, kvc // 2), BF16),
            pltpu.VMEM((2, tok, kvc // 2), F32),
            pltpu.VMEM((2, half - 1, tok, kvc // 2), F32),
            pltpu.VMEM((2, half - 1, tok, kvc // 2), F32),
            dma((2, n)), dma((2, n)), dma((2, n)), dma((2, n)),
            dma((2, 2 * n)), dma((2, 2 * n)),
            dma((half,)), dma((half,)), dma((2, half)), dma((2, half)),
            dma((2, n)), dma((2, n)), dma((n,)), dma((n,)),
            dma((4,)),
        ],
        compiler_params=pltpu.CompilerParams(
            collective_id=0, has_side_effects=True, vmem_limit_bytes=VMEM_LIMIT
        ),
    )(x, gain, w, docs)


def attention_kernel(
    group, q_ref, g_ref, k_ref, v_ref, docs_ref, doc_ref, att_ref, dq_ref, own_ref, far_ref, dk, dv,
    pst, dst, qst, gst,
):
    slots, tok = k_ref.shape[0], k_ref.shape[2]
    keys = slots * tok
    scale = HEAD ** (-0.5)
    k = k_ref[...].reshape(keys, HEAD)
    v = v_ref[...].reshape(keys, HEAD)
    row = lax.broadcasted_iota(jnp.int32, (tok, tok), 0)
    col = lax.broadcasted_iota(jnp.int32, (tok, tok), 1)
    mine = doc_ref[...]
    parts = [(docs_ref[0, 0:1, :] == mine) & (col <= row)]
    for j in range(1, slots):
        parts.append(docs_ref[j, 0:1, :] == mine)
    bias = jnp.concatenate([jnp.where(p, 1.0, 0.0).astype(F32) for p in parts], axis=1)
    allowed = bias > 0.5
    nt = (((1,), (1,)), ((), ()))
    tn = (((0,), (0,)), ((), ()))

    def head(h, carry):
        at = pl.ds(pl.multiple_of(h * HEAD, HEAD), HEAD)
        q = q_ref[:, at]
        g = g_ref[:, at]
        raw = lax.dot_general(q, k, nt, preferred_element_type=F32) * scale
        masked = jnp.where(allowed, raw, -1e30)
        top = jnp.max(masked, axis=1, keepdims=True)
        expo = jnp.where(allowed, jnp.exp(masked - top), 0.0)
        inv = 1.0 / jnp.sum(expo, axis=1, keepdims=True)
        att = (
            jnp.dot(expo.astype(BF16), v, preferred_element_type=F32) * inv
        ).astype(BF16)
        att_ref[:, at] = att
        delta = jnp.sum(g.astype(F32) * att.astype(F32), axis=1, keepdims=True)
        probs = expo * inv
        gp = lax.dot_general(g, v, nt, preferred_element_type=F32)
        ds = (probs * (gp - delta)).astype(BF16)
        rows = pl.ds(pl.multiple_of(h * tok, tok), tok)
        pst[rows, :] = probs.astype(BF16)
        dst[rows, :] = ds
        qst[rows, :] = q
        gst[rows, :] = g
        dq_ref[:, at] = (
            jnp.dot(ds, k, preferred_element_type=F32) * scale
        ).astype(BF16)
        return carry

    lax.fori_loop(0, group, head, 0, unroll=8)
    dv[...] = lax.dot_general(pst[...], gst[...], tn, preferred_element_type=F32)
    dk[...] = lax.dot_general(dst[...], qst[...], tn, preferred_element_type=F32)
    own_ref[0] = dk[0:tok, :] * scale
    own_ref[1] = dv[0:tok, :]
    for j in range(1, slots):
        far_ref[j - 1, 0] = (dk[j * tok : (j + 1) * tok, :] * scale).astype(BF16)
        far_ref[j - 1, 1] = dv[j * tok : (j + 1) * tok, :].astype(BF16)


def run_attention(q, g, kv, docs, doc_col):
    slots, _, tok, kvw = kv.shape
    heads = kvw // HEAD
    group = q.shape[1] // HEAD // heads
    gw = group * HEAD
    wide = pl.BlockSpec((tok, gw), lambda i: (0, i))
    return pl.pallas_call(
        functools.partial(attention_kernel, group),
        name="attention",
        grid=(heads,),
        out_shape=(
            jax.ShapeDtypeStruct(q.shape, BF16),
            jax.ShapeDtypeStruct(q.shape, BF16),
            jax.ShapeDtypeStruct((2, tok, kvw), F32),
            jax.ShapeDtypeStruct((slots - 1, 2, tok, kvw), BF16),
        ),
        in_specs=[
            wide,
            wide,
            pl.BlockSpec((slots, 1, tok, HEAD), lambda i: (0, 0, 0, i)),
            pl.BlockSpec((slots, 1, tok, HEAD), lambda i: (0, 1, 0, i)),
            pl.BlockSpec(docs.shape, lambda i: (0, 0, 0)),
            pl.BlockSpec(doc_col.shape, lambda i: (0, 0)),
        ],
        out_specs=(
            wide,
            wide,
            pl.BlockSpec((2, tok, HEAD), lambda i: (0, 0, i)),
            pl.BlockSpec((slots - 1, 2, tok, HEAD), lambda i: (0, 0, 0, i)),
        ),
        scratch_shapes=[
            pltpu.VMEM((slots * tok, HEAD), F32),
            pltpu.VMEM((slots * tok, HEAD), F32),
            pltpu.VMEM((group * tok, slots * tok), BF16),
            pltpu.VMEM((group * tok, slots * tok), BF16),
            pltpu.VMEM((group * tok, HEAD), BF16),
            pltpu.VMEM((group * tok, HEAD), BF16),
        ],
    )(q, g, kv, kv, docs, doc_col)


def backward_kernel(
    n, m, back,
    x_ref, gain_ref, cols_in, slab_in, own_ref, far_ref,
    dx_ref, dw_ref, dgain_ref,
    cols, slab, far_buf, gkv, nsend, nrecv, pair_send, pair_recv, keep, osend, orecv, seq_gain, blk_gain,
    psend, precv, gsend, grecv, asend, arecv, csend, crecv, wsend, wrecv, ssend, srecv, bsend, brecv, lsem,
):
    piece = dw_ref.shape[0]
    wide = cols.shape[2]
    half = m // 2
    s = lax.axis_index("seq")
    b = lax.axis_index("blk")
    core = lax.rem(b, 2)
    chip = b // 2
    partner = b + 1 - 2 * core
    tok, width = x_ref.shape
    kvw = own_ref.shape[2]
    loads = [
        pltpu.make_async_copy(cols_in, cols, lsem.at[0]),
        pltpu.make_async_copy(slab_in, slab, lsem.at[1]),
    ]
    for copy in loads:
        copy.start()
    greet(n, m)
    far_copies = []
    for h in range(2):
        far_copies.append([])
        for j in range(1, back + 1):
            copy = remote(
                far_ref.at[j - 1, h], far_buf.at[j - 1, h], psend.at[h, j], precv.at[h, j],
                seq=lax.rem(s - j + n, n),
            )
            far_copies[h].append(copy)

            @pl.when(s - j >= 0)
            def _(copy=copy):
                copy.start()

            @pl.when(s + j >= n)
            def _(j=j, h=h):
                far_buf[j - 1, h] = jnp.zeros(far_buf.shape[2:], BF16)

    inv = inverse_rms(x_ref)
    gather = []

    def sum_half(h):
        for j in range(1, back + 1):

            @pl.when(s + j < n)
            def _(j=j):
                far_copies[h][j - 1].wait_recv()

        total = own_ref[h]
        for j in range(1, back + 1):
            total = total + far_buf[j - 1, h].astype(F32)
        gkv[h, chip] = total.astype(BF16)
        for k in range(1, half):
            copy = remote(
                gkv.at[h, chip], gkv.at[h, chip], gsend.at[h, k], grecv.at[h, k],
                blk=lax.rem(b + 2 * k, m),
            )
            copy.start()
            gather.append(copy)

    tile = 256
    tiles = n * piece // tile

    def weight_tile(h, of_core, t):
        left = cols[:, :, lanes(of_core * tiles + t, tile)].reshape(half * tok, tile)
        return lax.dot_general(
            left, gkv[h].reshape(half * tok, kvw), (((0,), (0,)), ((), ())),
            preferred_element_type=F32,
        )

    pair_copies = [[], []]

    def weight_half(h):
        for k in range(1, half):
            source = lax.rem(chip - k + half, half)
            remote(
                gkv.at[h, chip], gkv.at[h, source], gsend.at[h, k], grecv.at[h, k],
                blk=lax.rem(b - 2 * k + m, m),
            ).wait_recv()
        for t in range(tiles):
            at = pl.ds(t * tile, tile)
            pair_send[h, at] = weight_tile(h, 1 - core, t).astype(BF16)
            copy = remote(
                pair_send.at[h, at], pair_recv.at[h, at], csend.at[h, t], crecv.at[h, t], blk=partner
            )
            copy.start()
            pair_copies[h].append(copy)

        def kept(t, carry):
            at = pl.ds(pl.multiple_of(t * tile, tile), tile)
            keep[h, at] = weight_tile(h, core, t)
            return carry

        lax.fori_loop(0, tiles, kept, 0)

    owner_copies = [[], []]

    def send_half(h):
        for copy in pair_copies[h]:
            copy.wait_recv()
        for j in far_first(n):
            target = lax.rem(s + j, n)
            at = pl.ds(pl.multiple_of(target * piece, piece), piece)
            osend[h, j - 1] = (keep[h, at] + pair_recv[h, at].astype(F32)).astype(BF16)
            copy = remote(
                osend.at[h, j - 1], orecv.at[h, j - 1], wsend.at[h, j], wrecv.at[h, j], seq=target
            )
            copy.start()
            owner_copies[h].append(copy)

    def to_normed(source, ref):
        def one(t, carry):
            rows = pl.ds(pl.multiple_of(t * 256, 256), 256)
            terms = [
                lax.dot_general(
                    gkv[h, source], slab[h, rows, :], (((1,), (1,)), ((), ())),
                    preferred_element_type=F32,
                )
                for h in range(2)
            ]
            ref[:, lanes(t, 256)] = (terms[0] + terms[1]).astype(BF16)
            return carry

        lax.fori_loop(0, wide // 256, one, 0)

    sum_half(0)
    for copy in loads:
        copy.wait()
    weight_half(0)
    sum_half(1)
    send_half(0)
    weight_half(1)
    normed_copies = []
    for k in range(1, half):
        source = lax.rem(chip - k + half, half)
        to_normed(source, nsend.at[k - 1])
        copy = remote(
            nsend.at[k - 1], nrecv.at[chip], asend.at[k], arecv.at[k], blk=lax.rem(b - 2 * k + m, m)
        )
        copy.start()
        normed_copies.append(copy)
    send_half(1)
    to_normed(chip, nrecv.at[chip])

    for k in range(1, half):
        source = lax.rem(chip + k, half)
        remote(
            nsend.at[k - 1], nrecv.at[source], asend.at[k], arecv.at[k], blk=lax.rem(b + 2 * k, m)
        ).wait_recv()

    per = wide // 256

    def means(i, total):
        at = lanes(i, 256)
        scaled = x_ref[:, at].astype(F32) * inv
        term = nrecv[i // per, :, lanes(lax.rem(i, per), 256)].astype(F32) * scaled
        blk_gain[b, pl.ds(i, 1), :] = jnp.sum(term, axis=0, keepdims=True)
        term = term * gain_ref[:, at]
        return total + term[:, :128] + term[:, 128:]

    total = lax.fori_loop(0, width // 256, means, jnp.zeros((tok, 128), F32), unroll=2)
    blk_copies = []
    for j in range(1, m):
        copy = remote(
            blk_gain.at[b], blk_gain.at[b], bsend.at[j], brecv.at[j], blk=lax.rem(b + j, m)
        )
        copy.start()
        blk_copies.append(copy)
    mean = jnp.sum(total, axis=1, keepdims=True) / width

    def finish(i, carry):
        at = lanes(i, 256)
        scaled = x_ref[:, at].astype(F32) * inv
        hat = nrecv[i // per, :, lanes(lax.rem(i, per), 256)].astype(F32) * gain_ref[:, at]
        dx_ref[:, at] = (inv * (hat - scaled * mean)).astype(BF16)
        return carry

    lax.fori_loop(0, width // 256, finish, 0, unroll=2)
    for j in range(1, m):
        source = lax.rem(b - j + m, m)
        remote(
            blk_gain.at[b], blk_gain.at[source], bsend.at[j], brecv.at[j], blk=source
        ).wait_recv()
    gain_sum = blk_gain[0]
    for i in range(1, m):
        gain_sum = gain_sum + blk_gain[i]
    seq_gain[s] = gain_sum
    seq_copies = []
    for j in range(1, n):
        copy = remote(
            seq_gain.at[s], seq_gain.at[s], ssend.at[j], srecv.at[j], seq=lax.rem(s + j, n)
        )
        copy.start()
        seq_copies.append(copy)

    at = pl.ds(pl.multiple_of(s * piece, piece), piece)
    for h in range(2):
        for copy in owner_copies[h]:
            copy.wait_recv()
        dw = keep[h, at] + pair_recv[h, at].astype(F32)
        for j in range(1, n):
            dw = dw + orecv[h, j - 1].astype(F32)
        dw_ref[:, h * kvw : (h + 1) * kvw] = dw
    for j in range(1, n):
        source = lax.rem(s - j + n, n)
        remote(
            seq_gain.at[s], seq_gain.at[source], ssend.at[j], srecv.at[j], seq=source
        ).wait_recv()
    gain_sum = seq_gain[0]
    for i in range(1, n):
        gain_sum = gain_sum + seq_gain[i]
    dgain_ref[...] = gain_sum
    for copy in (
        gather + normed_copies + pair_copies[0] + pair_copies[1]
        + owner_copies[0] + owner_copies[1] + seq_copies + blk_copies
    ):
        copy.wait_send()
    for j in range(1, back + 1):

        @pl.when(s - j >= 0)
        def _(j=j):
            far_copies[0][j - 1].wait_send()
            far_copies[1][j - 1].wait_send()


def run_backward(n, m, back, piece, x, gain, cols, slab, own, far):
    tok, width = x.shape
    _, wide, kvw = slab.shape
    kvc = 2 * kvw
    dma = pltpu.SemaphoreType.DMA
    vmem = pl.BlockSpec(memory_space=pltpu.VMEM)
    hbm = pl.BlockSpec(memory_space=pl.ANY)
    half = m // 2
    gains = (width // 256, 256)
    return pl.pallas_call(
        functools.partial(backward_kernel, n, m, back),
        name="backward_exchange",
        out_shape=(
            jax.ShapeDtypeStruct((tok, width), BF16),
            jax.ShapeDtypeStruct((piece, kvc), F32),
            jax.ShapeDtypeStruct(gains, F32),
        ),
        in_specs=[vmem, vmem, hbm, hbm, vmem, vmem],
        out_specs=(vmem, vmem, vmem),
        scratch_shapes=[
            pltpu.VMEM(cols.shape, BF16),
            pltpu.VMEM(slab.shape, BF16),
            pltpu.VMEM(far.shape, BF16),
            pltpu.VMEM((2, half, tok, kvw), BF16),
            pltpu.VMEM((half - 1, tok, wide), BF16),
            pltpu.VMEM((half, tok, wide), BF16),
            pltpu.VMEM((2, n * piece, kvw), BF16),
            pltpu.VMEM((2, n * piece, kvw), BF16),
            pltpu.VMEM((2, n * piece, kvw), F32),
            pltpu.VMEM((2, n - 1, piece, kvw), BF16),
            pltpu.VMEM((2, n - 1, piece, kvw), BF16),
            pltpu.VMEM((n,) + gains, F32),
            pltpu.VMEM((m,) + gains, F32),
            dma((2, n)), dma((2, n)), dma((2, half)), dma((2, half)), dma((half,)), dma((half,)),
            dma((2, n)), dma((2, n)), dma((2, n)), dma((2, n)),
            dma((n,)), dma((n,)), dma((m,)), dma((m,)),
            dma((2,)),
        ],
        compiler_params=pltpu.CompilerParams(
            collective_id=1, has_side_effects=True, vmem_limit_bytes=VMEM_LIMIT
        ),
    )(x, gain, cols, slab, own, far)


def shards(layer_input, queries, grad_out, segment_ids, kv_weight, norm_gain):
    n, m = lax.axis_size("seq"), lax.axis_size("blk")
    tok = layer_input.shape[1]
    back = max(n // 2, 1)
    x = layer_input[0]
    gain = norm_gain[None]
    docs = jnp.broadcast_to(segment_ids, (8, tok))
    doc_col = jnp.broadcast_to(segment_ids[0][:, None], (tok, tok))
    cols, slab, kv, all_docs = run_forward(n, m, back, x, gain, kv_weight, docs)
    attended, grad_queries, own, far = run_attention(
        queries[0], grad_out[0], kv, all_docs, doc_col
    )
    dx, dw, dgain = run_backward(
        n, m, back, kv_weight.shape[0], x, gain, cols, slab, own, far
    )
    return attended[None], grad_queries[None], dx[None], dw, dgain.reshape(-1)


def solution(mesh):
    tokens = P("blk", "seq", None)
    rows = P(("blk", "seq"), None)
    return jax.shard_map(
        shards,
        mesh=mesh,
        in_specs=(tokens, tokens, tokens, P("blk", "seq"), rows, P()),
        out_specs=(tokens, tokens, tokens, rows, P()),
        check_vma=False,
    )
```
